32 devices in a mesh: tower: 2 (over x), dp: 16 (over z, y, core).
Axes of the slice: x: 2, y: 2, z: 4, core: 2. Of those that a mesh axis runs over, the one named last changes fastest.
Arguments:
- tokens: bfloat16 [2, 16384, 768], P('tower', 'dp'), may hold values from -6 to 6
- segments: int32 [2, 128, 128], P('tower', 'dp'), may hold values from 0 to 7, as said below
- pairs: int32 [1024], replicated, may hold values from 0 to 1023, as said below
- scores: float32 [1024], replicated, may hold values from -0.5 to 1
- w_qkv: bfloat16 [768, 2304], replicated, may hold values from -0.21875 to 0.21875
- b_query: float32 [768], replicated, may hold values from -1.75 to 1.75
- b_value: float32 [768], replicated, may hold values from -3 to 3
- w_out: bfloat16 [768, 768], replicated, may hold values from -0.4375 to 0.4375
- b_out: float32 [768], replicated, may hold values from -3 to 3
- gain_one: float32 [768], replicated, may hold values from 0.25 to 1.75
- shift_one: float32 [768], replicated, may hold values from -1.25 to 1.25
- w_in: bfloat16 [768, 3072], replicated, may hold values from -0.21875 to 0.21875
- b_in: float32 [3072], replicated, may hold values from -3 to 3
- w_down: bfloat16 [3072, 768], replicated, may hold values from -0.109375 to 0.109375
- b_down: float32 [768], replicated, may hold values from -3 to 3
- gain_two: float32 [768], replicated, may hold values from 0.25 to 1.75
- shift_two: float32 [768], replicated, may hold values from -0.625 to 0.625
Outputs:
- output_rows: bfloat16 [2, 16384, 768], P('tower', 'dp')
- grad_tokens: float32 [2, 16384, 768], P('tower', 'dp')
- grad_w_qkv: float32 [768, 2304], replicated
- grad_b_query: float32 [768], replicated
- grad_b_value: float32 [768], replicated
- grad_w_out: float32 [768, 768], replicated
- grad_b_out: float32 [768], replicated
- grad_gain_one: float32 [768], replicated
- grad_shift_one: float32 [768], replicated
- grad_w_in: float32 [768, 3072], replicated
- grad_b_in: float32 [3072], replicated
- grad_w_down: float32 [3072, 768], replicated
- grad_b_down: float32 [768], replicated
- grad_gain_two: float32 [768], replicated
- grad_shift_two: float32 [768], replicated
The draws below stay inside these ranges and needn't reach their ends.
Inputs may be any that keep to these rules, and one draw needn't show every extreme that they name: `segments`: within each packed row the numbers never fall along the row and run from 0 to 7, each one present. `pairs`: every B sentence is the partner of exactly one A sentence.
All inputs are finite; a program needn't handle non-finite values.
Results may differ from the reference program's by a relative error of at most 0.008.
Values may be sent and summed in bfloat16 or wider, within the bound.
No kernel may reach another device: no remote copies, remote signals or barrier semaphores. Data moves between devices by JAX's collectives and lax.ppermute only.
A program may use at most 256 MiB of HBM per device.

```python
import math
from functools import partial
import jax
import jax.numpy as jnp
from jax import lax

D = 768
HEADS = 12
HEAD_DIM = 64
FF = 3072
ROW_LEN = 128
SEG_ROW = 8
ROWS_DEV = 8
ROWS_ALL = 128
TOKENS = 16384
NPAIRS = 1024


def draw_segments(key, part):
    row_keys = jax.random.split(key, 2 * ROWS_ALL)

    def cuts_of(row_key):
        return jax.random.permutation(row_key, ROW_LEN - 1)[:SEG_ROW - 1] + 1
    cut_points = jax.vmap(cuts_of)(row_keys).astype(jnp.int32)
    positions = jnp.arange(ROW_LEN, dtype=jnp.int32)
    seg_ids = jnp.sum((positions[None, :, None] >= cut_points[:, None, :]).astype(jnp.int32), -1)
    return seg_ids.reshape(2, ROWS_ALL, ROW_LEN).astype(jnp.int32)


def draw_pairs(key, part):
    slots = ROWS_DEV * SEG_ROW
    owners = NPAIRS // slots
    slot_key = jax.random.fold_in(key, 11)
    order_key = jax.random.fold_in(key, 12)
    extra_key = jax.random.fold_in(key, 13)
    target_slot = jax.random.permutation(slot_key, slots).astype(jnp.int32)
    extra = jax.random.randint(extra_key, (slots,), 0, owners).astype(jnp.int32)
    fixed = jnp.array([0, owners - 1, 1, owners // 2], jnp.int32)
    offsets = jnp.concatenate([fixed, extra[4:]], 0)
    offsets = jax.random.permutation(order_key, offsets).astype(jnp.int32)
    owner_ids = jnp.arange(owners, dtype=jnp.int32)
    partner_owner = (owner_ids[:, None] + offsets[None, :]) % owners
    result = partner_owner * slots + target_slot[None, :]
    return result.reshape(NPAIRS).astype(jnp.int32)


def shard_levels(key, shape, cuts, smallest, high):
    loudness = 1.0
    for dim, blocks in cuts:
        draws = jax.random.uniform(jax.random.fold_in(jax.random.fold_in(key, 6), dim), (blocks,), jnp.float32, smallest / len(cuts), high / len(cuts))
        loudness = loudness * jnp.repeat(jnp.exp(draws), shape[dim] // blocks).reshape((-1,) + (1,) * (len(shape) - 1 - dim))
    return loudness


def gaussian(own_key, extent, scale, most, pieces=(), kind=jnp.bfloat16):
    level = shard_levels(own_key, extent, pieces, -0.22, 0.18) if pieces else 1.0
    drawn = jax.random.normal(own_key, extent, jnp.float32) * scale * level
    return jnp.minimum(jnp.maximum(drawn, -most), most).astype(kind)


def setup_inputs(seed: int = 0) -> dict:
    splits = jax.random.split(jax.random.key(seed), 18)
    return {
        "tokens": gaussian(splits[0], (2, TOKENS, D), 1.0, 6.0, ((0, 2), (1, 16))),
        "segments": draw_segments(jax.random.fold_in(splits[17], 71), 0),
        "pairs": draw_pairs(jax.random.fold_in(splits[17], 71), 0),
        "scores": jnp.clip(jax.random.uniform(splits[3], (NPAIRS,), jnp.float32, -0.5, 1.0), -0.5, 1.0),
        "w_qkv": gaussian(splits[4], (D, 3 * D), D ** -0.5, 0.21875),
        "b_query": gaussian(splits[5], (D,), 0.3, 1.75, (), jnp.float32),
        "b_value": gaussian(splits[6], (D,), 0.5, 3.0, (), jnp.float32),
        "w_out": gaussian(splits[7], (D, D), (D // 4) ** -0.5, 0.4375),
        "b_out": gaussian(splits[8], (D,), 0.5, 3.0, (), jnp.float32),
        "gain_one": jnp.clip(1.0 + 0.15 * jax.random.normal(splits[9], (D,), jnp.float32), 0.25, 1.75),
        "shift_one": gaussian(splits[10], (D,), 0.2, 1.25, (), jnp.float32),
        "w_in": gaussian(splits[11], (D, FF), D ** -0.5, 0.21875),
        "b_in": gaussian(splits[12], (FF,), 0.5, 3.0, (), jnp.float32),
        "w_down": gaussian(splits[13], (FF, D), FF ** -0.5, 0.109375),
        "b_down": gaussian(splits[14], (D,), 0.5, 3.0, (), jnp.float32),
        "gain_two": jnp.clip(1.0 + 0.15 * jax.random.normal(splits[15], (D,), jnp.float32), 0.25, 1.75),
        "shift_two": gaussian(splits[16], (D,), 0.1, 0.625, (), jnp.float32),
    }


loss_scale = 65536.0

@jax.custom_vjp
def low(v):
    return lax.optimization_barrier(v.astype(jnp.bfloat16)).astype(jnp.float32)

@jax.custom_vjp
def low_back(v):
    return v

def low_keep(v):
    return (low(v), None)

def low_pass(kept, grad):
    return (grad,)

def back_keep(v):
    return (v, None)

def back_low(kept, grad):
    return (low(grad),)
low.defvjp(low_keep, low_pass)
low_back.defvjp(back_keep, back_low)

def product(left, right):
    return jnp.dot(left, right, precision=lax.Precision.HIGHEST)

def layer_norm(values_in, gain_vec, shift_vec):
    row_mean = lax.optimization_barrier(jnp.mean(values_in, -1, keepdims=True))
    centered = values_in - row_mean
    variance = lax.optimization_barrier(jnp.mean(centered * centered, -1, keepdims=True))
    return centered * lax.rsqrt(variance + 1e-12) * gain_vec + shift_vec

def layer_rows(params, block):
    token_rows, seg_rows = block
    w_qkv, b_query, b_value, w_out, b_out, gain_one, shift_one, w_in, b_in, w_down, b_down, gain_two, shift_two = params
    row_count = token_rows.shape[0]
    flat_rows = token_rows.reshape(row_count * ROW_LEN, D)
    joint_rows = low_back(product(flat_rows, w_qkv))
    head_shape = (row_count, ROW_LEN, HEADS, HEAD_DIM)
    query_rows = low(joint_rows[:, :D] + b_query).reshape(head_shape)
    key_rows = low(joint_rows[:, D:2 * D]).reshape(head_shape)
    value_rows = low(joint_rows[:, 2 * D:] + b_value).reshape(head_shape)
    score_scale = 1.0 / math.sqrt(HEAD_DIM)
    raw_scores = low_back(jnp.einsum('rqhd,rkhd->rhqk', query_rows, key_rows, precision=lax.Precision.HIGHEST) * score_scale)
    same_segment = (seg_rows[:, :, None] == seg_rows[:, None, :])[:, None]
    masked = jnp.where(same_segment, raw_scores, -1e+30)
    attn_weights = low(jax.nn.softmax(masked, axis=-1))
    context = low(low_back(jnp.einsum('rhqk,rkhd->rqhd', attn_weights, value_rows, precision=lax.Precision.HIGHEST)))
    context = context.reshape(row_count * ROW_LEN, D)
    attended = low_back(product(context, w_out)) + b_out
    hidden = layer_norm(flat_rows + attended, gain_one, shift_one)
    up_rows = low_back(product(low(hidden), w_in)) + b_in
    activated = low(jax.nn.gelu(up_rows, approximate=False))
    down_rows = low_back(product(activated, w_down)) + b_down
    output_rows = layer_norm(hidden + down_rows, gain_two, shift_two)
    onehot = (seg_rows[:, :, None] == jnp.arange(SEG_ROW, dtype=jnp.int32)[None, None, :]).astype(jnp.float32)
    counts = lax.optimization_barrier(jnp.sum(onehot, 1))
    seg_sums = jnp.einsum('rts,rtd->rsd', onehot, output_rows.reshape(row_count, ROW_LEN, D), precision=lax.Precision.HIGHEST)
    pooled = (seg_sums / counts[:, :, None]).reshape(row_count * SEG_ROW, D)
    return (output_rows.reshape(row_count, ROW_LEN, D), pooled)

def forward(token_all, params, segments, pairs, scores):
    row_total = 2 * ROWS_ALL
    block_rows = math.gcd(row_total, 32)
    blocks = row_total // block_rows
    token_blocks = token_all.reshape(blocks, block_rows, ROW_LEN, D)
    seg_blocks = segments.reshape(blocks, block_rows, ROW_LEN)
    step_fn = jax.checkpoint(partial(layer_rows, params))
    output_rows, pooled = lax.map(step_fn, (token_blocks, seg_blocks))
    pooled_low = low(pooled.reshape(2, NPAIRS, D))
    first_side = pooled_low[0]
    second_side = pooled_low[1][pairs]
    inv_first = lax.rsqrt(lax.optimization_barrier(jnp.sum(first_side * first_side, -1)) + 1e-06)
    inv_second = lax.rsqrt(lax.optimization_barrier(jnp.sum(second_side * second_side, -1)) + 1e-06)
    cosine = lax.optimization_barrier(jnp.sum(first_side * second_side, -1)) * inv_first * inv_second
    differ = cosine - scores
    loss = loss_scale * jnp.mean(differ * differ)
    return (loss, output_rows.reshape(2, TOKENS, D))

def reference(tokens, segments, pairs, scores, w_qkv, b_query, b_value, w_out, b_out, gain_one, shift_one, w_in, b_in, w_down, b_down, gain_two, shift_two):
    params = tuple((weight_arg.astype(jnp.float32) for weight_arg in (w_qkv, b_query, b_value, w_out, b_out, gain_one, shift_one, w_in, b_in, w_down, b_down, gain_two, shift_two)))

    def objective(token_all, weights):
        return forward(token_all, weights, segments, pairs, scores)
    loss, pullback, output_rows = jax.vjp(objective, tokens.astype(jnp.float32), params, has_aux=True)
    grad_tokens, grads = pullback(jnp.ones((), jnp.float32))
    return (output_rows.astype(jnp.bfloat16), grad_tokens, grads[0], grads[1], grads[2], grads[3], grads[4], grads[5], grads[6], grads[7], grads[8], grads[9], grads[10], grads[11], grads[12])
```

```python
import math
from functools import partial

import jax
import jax.numpy as jnp
from jax import lax
from jax.experimental import pallas as pl
from jax.experimental.pallas import tpu as pltpu
from jax.sharding import PartitionSpec as P

HEADS = 12
SEG_ROW = 8
AXES = ("tower", "dp")
HOPS = ((8, 2, 4, 1), (1, 8, 2, 4))
POOL_HOPS = ((1, 4, 2), (4, 2, 1))

loss_scale = 65536.0
f32 = jnp.float32
bf16 = jnp.bfloat16
LIMIT = 56 << 20


def call_params():
    return pltpu.CompilerParams(vmem_limit_bytes=LIMIT)


def hop_pairs(dp_size, flip):
    result = []
    for device in range(2 * dp_size):
        tower, place = divmod(device, dp_size)
        tower_bit, place_bits = flip(place & 1)
        result.append((device, (tower ^ tower_bit) * dp_size + (place ^ place_bits)))
    return result


def swap_hop(value, dp_size, masks):
    pairs = hop_pairs(dp_size, lambda core: (masks[core] >> 3, (masks[core] & 7) << 1))
    return lax.ppermute(value, AXES, pairs)


def swap_core(value, dp_size):
    return lax.ppermute(value, AXES, hop_pairs(dp_size, lambda core: (0, 1)))


def swap_place(value, dp_size, bits):
    return lax.ppermute(value, AXES, hop_pairs(dp_size, lambda core: (0, bits)))


def span(masks):
    result = [0]
    for mask in reversed(masks):
        result = result + [mask ^ entry for entry in result]
    return result


def place_tables(dp_size):
    tower = lax.axis_index("tower")
    place = lax.axis_index("dp")
    core = place & 1
    unit = (tower << 3) | ((place >> 1) & 7)
    lists = []
    for hops in HOPS:
        order = span(hops)
        lists.append([order.index(mask) for mask in range(16)])
    inverse = jnp.array(lists, jnp.int32)
    rows = inverse[:, unit ^ jnp.arange(16, dtype=jnp.int32)]
    return core, jnp.where(core == 0, rows, rows[::-1])


def grad_half(terms, half, table, kind, small=None):
    count = terms[0][0].shape[0]
    rows = terms[0][0].shape[1]
    block = rows // 16
    tile = min(rows, 8 * block, 768)
    per_tile = tile // block
    widths = [rhs.shape[1] // 2 for _, rhs in terms]
    total = sum(widths) + (128 if small is not None else 0)
    meta = jnp.concatenate([half[None], table])

    def body(meta_ref, *refs):
        out_ref = refs[-1]
        step = pl.program_id(0)
        start = 0
        for index, width in enumerate(widths):
            part = lax.dot_general(
                refs[2 * index][...],
                refs[2 * index + 1][...],
                (((0,), (0,)), ((), ())),
                preferred_element_type=f32,
            ).astype(kind)
            for inner in range(per_tile):
                spot = meta_ref[1 + step * per_tile + inner]
                out_ref[spot, :, start : start + width] = part[inner * block : (inner + 1) * block]
            start += width
        if small is not None:
            for inner in range(per_tile):
                spot = meta_ref[1 + step * per_tile + inner]
                extra = refs[2 * len(widths)][0, step * per_tile + inner]
                out_ref[spot, :, start : start + 128] = jnp.concatenate(
                    [extra, jnp.zeros((block - extra.shape[0], 128), f32)], 0
                ).astype(kind)

    in_specs = []
    operands = []
    for (lhs, rhs), width in zip(terms, widths):
        in_specs.append(pl.BlockSpec((count, tile), lambda step, meta_ref: (0, step)))
        in_specs.append(pl.BlockSpec((count, width), lambda step, meta_ref: (0, meta_ref[0])))
        operands += [lhs, rhs]
    if small is not None:
        in_specs.append(
            pl.BlockSpec((1,) + small.shape[1:], lambda step, meta_ref: (meta_ref[0], 0, 0, 0))
        )
        operands.append(small)
    return pl.pallas_call(
        body,
        out_shape=jax.ShapeDtypeStruct((16, block, total), kind),
        grid_spec=pltpu.PrefetchScalarGridSpec(
            num_scalar_prefetch=1,
            grid=(rows // tile,),
            in_specs=in_specs,
            out_specs=pl.BlockSpec((16, block, total), lambda step, meta_ref: (0, 0, 0)),
        ),
        compiler_params=call_params(),
        cost_estimate=pl.CostEstimate(
            flops=2 * count * rows * sum(widths),
            bytes_accessed=2 * count * (len(widths) * rows + sum(widths)) + 3 * rows * total,
            transcendentals=0,
        ),
    )(meta, *operands)


def finish(mine, theirs, core, table, widths, small_rows=0):
    block = mine.shape[1]
    rows = 16 * block
    tiles = 4
    per_tile = 16 // tiles
    meta = jnp.concatenate([core[None], table.reshape(32)])

    def body(meta_ref, mine_ref, theirs_ref, *outs):
        step = pl.program_id(0)

        def fill(first_ref, first_at, second_ref, second_at):
            for inner in range(per_tile):
                number = step * per_tile + inner
                first = meta_ref[first_at + number]
                second = meta_ref[second_at + number]
                start = 0
                for out_ref, width in zip(outs, widths):
                    lines = slice(inner * block, (inner + 1) * block)
                    out_ref[lines, :width] = first_ref[first, :, start : start + width].astype(f32)
                    out_ref[lines, width:] = second_ref[second, :, start : start + width].astype(
                        f32
                    )
                    start += width
                if small_rows:
                    lines = slice(start, start + 128)
                    outs[-1][0, number] = first_ref[first, :, lines].astype(f32)[:small_rows]
                    outs[-1][1, number] = second_ref[second, :, lines].astype(f32)[:small_rows]

        @pl.when(meta_ref[0] == 0)
        def _():
            fill(mine_ref, 1, theirs_ref, 17)

        @pl.when(meta_ref[0] != 0)
        def _():
            fill(theirs_ref, 17, mine_ref, 1)

    whole = pl.BlockSpec(mine.shape, lambda step, meta_ref: (0, 0, 0))
    out_shape = [jax.ShapeDtypeStruct((rows, 2 * width), f32) for width in widths]
    out_specs = [
        pl.BlockSpec((rows // tiles, 2 * width), lambda step, meta_ref: (step, 0))
        for width in widths
    ]
    if small_rows:
        out_shape.append(jax.ShapeDtypeStruct((2, 16, small_rows, 128), f32))
        out_specs.append(
            pl.BlockSpec((2, 16, small_rows, 128), lambda step, meta_ref: (0, 0, 0, 0))
        )
    return pl.pallas_call(
        body,
        out_shape=out_shape,
        grid_spec=pltpu.PrefetchScalarGridSpec(
            num_scalar_prefetch=1, grid=(tiles,), in_specs=[whole, whole], out_specs=out_specs
        ),
        compiler_params=call_params(),
        cost_estimate=pl.CostEstimate(
            flops=0, bytes_accessed=6 * mine.size * 2, transcendentals=0
        ),
    )(meta, mine, theirs)


def sum_over_all(sent, kept, dp_size):
    terms = [kept, swap_core(sent, dp_size)]

    def piece(start, stop):
        return sum(term[start:stop].astype(f32) for term in terms)

    size = 16
    for hop in range(4):
        size //= 2
        part = piece(size, 2 * size).astype(bf16)
        terms.append(swap_hop(part, dp_size, (HOPS[0][hop], HOPS[1][hop])))
    own = piece(0, 1)
    bits = 16
    while bits < dp_size:
        own = own + swap_place(own.astype(bf16), dp_size, bits).astype(f32)
        bits *= 2
    whole = own.astype(bf16)
    for hop in (3, 2, 1, 0):
        whole = jnp.concatenate(
            [whole, swap_hop(whole, dp_size, (HOPS[0][hop], HOPS[1][hop]))], 0
        )
    return whole, swap_core(whole, dp_size)


def gather_pooled(pooled_low, dp_size):
    place = lax.axis_index("dp")
    core = place & 1
    rows = lax.ppermute(pooled_low, "tower", [(0, 1), (1, 0)])[None]
    extra = []
    bits = 8
    while 2 * bits < dp_size:
        extra.append(bits)
        bits *= 2
    orders = [list(hops) + extra for hops in POOL_HOPS]
    spans = [[0], [0]]
    for first, second in zip(*orders):
        rows = jnp.concatenate(
            [rows, swap_hop(rows, dp_size, (first, second))]
            if max(first, second) < 8
            else [rows, swap_place(rows, dp_size, 2 * first)],
            0,
        )
        spans = [
            entry + [mask ^ old for old in entry] for entry, mask in zip(spans, (first, second))
        ]
    other = swap_core(rows, dp_size)
    spans = jnp.array(spans, jnp.int32) << 1
    owner = jnp.stack([place ^ spans[0], place ^ 1 ^ spans[1]])
    owner_other = jnp.stack([place ^ spans[1], place ^ 1 ^ spans[0]])
    owner = jnp.where(core == 0, owner, owner_other).reshape(-1)
    return jnp.concatenate([rows, other], 0), owner


def gelu_exact(values_in):
    return jax.nn.gelu(values_in, approximate=False)


def layer_norm(values_in, gain_vec, shift_vec):
    row_mean = jnp.mean(values_in, -1, keepdims=True)
    centered = values_in - row_mean
    inv_std = lax.rsqrt(jnp.mean(centered * centered, -1, keepdims=True) + 1e-12)
    normed = centered * inv_std
    return (normed * gain_vec + shift_vec, normed, inv_std)


def norm_back(gradient, normed, inv_std, gain_vec):
    scaled = gradient * gain_vec
    inner = (
        scaled
        - jnp.mean(scaled, -1, keepdims=True)
        - normed * jnp.mean(scaled * normed, -1, keepdims=True)
    )
    return (inner * inv_std, jnp.sum(gradient * normed, 0), jnp.sum(gradient, 0))


def on_device(
    tokens,
    segments,
    pairs,
    scores,
    w_qkv,
    b_query,
    b_value,
    w_out,
    b_out,
    gain_one,
    shift_one,
    w_in,
    b_in,
    w_down,
    b_down,
    gain_two,
    shift_two,
):
    dp_size = lax.axis_size("dp")
    core, table = place_tables(dp_size)
    flat_rows = tokens[0]
    seg_rows = segments[0]
    row_count = seg_rows.shape[0]
    row_len = seg_rows.shape[1]
    model_width = flat_rows.shape[1]
    token_count = flat_rows.shape[0]
    head_dim = model_width // HEADS
    head_shape = (row_count, row_len, HEADS, head_dim)
    score_scale = 1.0 / math.sqrt(head_dim)
    joint_rows = jnp.dot(flat_rows, w_qkv, preferred_element_type=f32)
    query_rows = (joint_rows[:, :model_width] + b_query).astype(bf16).reshape(head_shape)
    key_rows = joint_rows[:, model_width : 2 * model_width].astype(bf16).reshape(head_shape)
    value_rows = (joint_rows[:, 2 * model_width :] + b_value).astype(bf16).reshape(head_shape)
    same_segment = (seg_rows[:, :, None] == seg_rows[:, None, :])[:, None]

    def score_of():
        raw = (
            jnp.einsum("rqhd,rkhd->rhqk", query_rows, key_rows, preferred_element_type=f32)
            * score_scale
        )
        return jnp.where(same_segment, raw, -1e30)

    scores_now = score_of()
    row_max = jnp.max(scores_now, -1, keepdims=True)
    expo = jnp.exp(scores_now - row_max)
    denom = jnp.sum(expo, -1, keepdims=True)
    log_total = row_max + jnp.log(denom)
    attn_low = (expo / denom).astype(bf16)
    context = jnp.einsum("rhqk,rkhd->rqhd", attn_low, value_rows, preferred_element_type=f32)
    context = context.astype(bf16).reshape(token_count, model_width)
    attended = jnp.dot(context, w_out, preferred_element_type=f32) + b_out
    hidden, normed_one, inv_std_one = layer_norm(
        flat_rows.astype(f32) + attended, gain_one, shift_one
    )
    hidden_low = hidden.astype(bf16)
    up_rows = jnp.dot(hidden_low, w_in, preferred_element_type=f32) + b_in
    gelu_value, gelu_back = jax.vjp(gelu_exact, up_rows)
    activated = gelu_value.astype(bf16)
    down_rows = jnp.dot(activated, w_down, preferred_element_type=f32) + b_down
    output_rows, normed_two, inv_std_two = layer_norm(hidden + down_rows, gain_two, shift_two)
    onehot = (seg_rows[:, :, None] == jnp.arange(SEG_ROW, dtype=jnp.int32)[None, None, :]).astype(
        f32
    )
    counts = jnp.sum(onehot, 1)
    seg_sums = jnp.einsum(
        "rts,rtd->rsd",
        onehot,
        output_rows.reshape(row_count, row_len, model_width),
        precision=lax.Precision.HIGHEST,
    )
    seg_count = row_count * SEG_ROW
    pooled_low = (seg_sums / counts[:, :, None]).reshape(seg_count, model_width).astype(bf16)
    tower_index = lax.axis_index("tower")
    row_block = lax.axis_index("dp")
    pair_count = pairs.shape[0]
    everyone, owner = gather_pooled(pooled_low, dp_size)
    own_start = row_block * seg_count
    own_index = own_start + jnp.arange(seg_count, dtype=jnp.int32)
    slots = jnp.arange(seg_count, dtype=jnp.int32)
    there = (owner[:, None] * seg_count + slots[None, :]).reshape(-1)
    pairs_there = pairs.reshape(-1, seg_count)[owner].reshape(-1)
    scores_there = scores.reshape(-1, seg_count)[owner].reshape(-1)
    pairs_here = lax.dynamic_slice_in_dim(pairs, own_start, seg_count)
    scores_here = lax.dynamic_slice_in_dim(scores, own_start, seg_count)
    on_first = tower_index == 0
    is_pair = (
        jnp.where(on_first, pairs_here, own_index)[:, None]
        == jnp.where(on_first, there, pairs_there)[None, :]
    )
    target = jnp.where(
        on_first, scores_here, jnp.sum(jnp.where(is_pair, scores_there[None, :], 0.0), 1)
    )
    partner = jnp.dot(
        is_pair.astype(bf16),
        everyone.reshape(pair_count, model_width),
        preferred_element_type=f32,
    )
    mine = pooled_low.astype(f32)
    inv_mine = lax.rsqrt(jnp.sum(mine * mine, -1) + 1e-06)
    inv_partner = lax.rsqrt(jnp.sum(partner * partner, -1) + 1e-06)
    cosine = jnp.sum(mine * partner, -1) * inv_mine * inv_partner
    coeff = loss_scale * 2.0 * (cosine - target) / pair_count
    d_pooled = coeff[:, None] * (
        partner * (inv_mine * inv_partner)[:, None] - (cosine * inv_mine * inv_mine)[:, None] * mine
    )
    per_token = d_pooled.reshape(row_count, SEG_ROW, model_width) / counts[:, :, None]
    d_output = jnp.einsum(
        "rts,rsd->rtd", onehot, per_token, precision=lax.Precision.HIGHEST
    ).reshape(token_count, model_width)
    d_mid, grad_gain_two, grad_shift_two = norm_back(d_output, normed_two, inv_std_two, gain_two)
    grad_b_down = jnp.sum(d_mid, 0)
    d_mid_low = d_mid.astype(bf16)
    down_terms = [(activated, d_mid_low)]
    down_sum = sum_over_all(
        grad_half(down_terms, 1 - core, table[1], bf16),
        grad_half(down_terms, core, table[0], f32),
        dp_size,
    )
    d_act = jnp.einsum("nd,fd->nf", d_mid_low, w_down, preferred_element_type=f32)
    d_up = gelu_back(d_act)[0]
    grad_b_in = jnp.sum(d_up, 0)
    d_up_low = d_up.astype(bf16)
    d_hidden = d_mid + jnp.einsum("nf,df->nd", d_up_low, w_in, preferred_element_type=f32)
    d_first, grad_gain_one, grad_shift_one = norm_back(d_hidden, normed_one, inv_std_one, gain_one)
    grad_b_out = jnp.sum(d_first, 0)
    d_first_low = d_first.astype(bf16)
    in_terms = [(hidden_low, d_up_low), (context, d_first_low)]
    in_sum = sum_over_all(
        grad_half(in_terms, 1 - core, table[1], bf16),
        grad_half(in_terms, core, table[0], f32),
        dp_size,
    )
    d_context = jnp.einsum("nd,cd->nc", d_first_low, w_out, preferred_element_type=f32)
    d_context = d_context.astype(bf16).reshape(head_shape)
    attn_again = jnp.exp(score_of() - log_total)
    attn_again_low = attn_again.astype(bf16)
    d_values = jnp.einsum("rhqk,rqhd->rkhd", attn_again_low, d_context, preferred_element_type=f32)
    d_attn = jnp.einsum("rqhd,rkhd->rhqk", d_context, value_rows, preferred_element_type=f32)
    d_scores = attn_again * (d_attn - jnp.sum(attn_again * d_attn, -1, keepdims=True))
    d_scores_low = d_scores.astype(bf16)
    d_query = (
        jnp.einsum("rhqk,rkhd->rqhd", d_scores_low, key_rows, preferred_element_type=f32)
        * score_scale
    )
    d_keys = (
        jnp.einsum("rhqk,rqhd->rkhd", d_scores_low, query_rows, preferred_element_type=f32)
        * score_scale
    )
    d_query = d_query.reshape(token_count, model_width)
    d_keys = d_keys.reshape(token_count, model_width)
    d_values = d_values.reshape(token_count, model_width)
    grad_b_query = jnp.sum(d_query, 0)
    grad_b_value = jnp.sum(d_values, 0)
    d_joint = jnp.concatenate([d_query, d_keys, d_values], -1).astype(bf16)
    small = jnp.concatenate(
        [
            grad_b_query,
            grad_b_value,
            grad_b_out,
            grad_gain_one,
            grad_shift_one,
            grad_b_in,
            grad_b_down,
            grad_gain_two,
            grad_shift_two,
        ]
    )
    small_count = small.shape[0]
    small_rows = -(-small_count // (32 * 128))
    small = jnp.pad(small, (0, 32 * 128 * small_rows - small_count))
    small = small.reshape(2, 16, small_rows, 128)
    qkv_terms = [(flat_rows, d_joint)]
    qkv_sum = sum_over_all(
        grad_half(qkv_terms, 1 - core, table[1], bf16, small),
        grad_half(qkv_terms, core, table[0], f32, small),
        dp_size,
    )
    grad_tokens = d_first + jnp.einsum("ne,de->nd", d_joint, w_qkv, preferred_element_type=f32)
    ff_width = w_in.shape[1]
    (grad_w_down,) = finish(*down_sum, core, table, [model_width // 2])
    grad_w_in, grad_w_out = finish(*in_sum, core, table, [ff_width // 2, model_width // 2])
    grad_w_qkv, small = finish(*qkv_sum, core, table, [3 * model_width // 2], small_rows)
    small = small.reshape(-1)
    pieces = []
    start = 0
    for length in [model_width] * 5 + [ff_width] + [model_width] * 3:
        pieces.append(lax.slice_in_dim(small, start, start + length))
        start += length
    (
        grad_b_query,
        grad_b_value,
        grad_b_out,
        grad_gain_one,
        grad_shift_one,
        grad_b_in,
        grad_b_down,
        grad_gain_two,
        grad_shift_two,
    ) = pieces
    return (
        output_rows.astype(bf16)[None],
        grad_tokens[None],
        grad_w_qkv,
        grad_b_query,
        grad_b_value,
        grad_w_out,
        grad_b_out,
        grad_gain_one,
        grad_shift_one,
        grad_w_in,
        grad_b_in,
        grad_w_down,
        grad_b_down,
        grad_gain_two,
        grad_shift_two,
    )


def solution(mesh):
    return jax.shard_map(
        on_device,
        mesh=mesh,
        in_specs=(
            P("tower", "dp", None),
            P("tower", "dp", None),
            P(),
            P(),
            P(),
            P(),
            P(),
            P(),
            P(),
            P(),
            P(),
            P(),
            P(),
            P(),
            P(),
            P(),
            P(),
        ),
        out_specs=(
            P("tower", "dp", None),
            P("tower", "dp", None),
            P(),
            P(),
            P(),
            P(),
            P(),
            P(),
            P(),
            P(),
            P(),
            P(),
            P(),
            P(),
            P(),
        ),
        check_vma=False,
    )
```

```python
import math
from functools import partial

import jax
import jax.numpy as jnp
from jax import lax
from jax.experimental import pallas as pl
from jax.experimental.pallas import tpu as pltpu
from jax.sharding import PartitionSpec as P

HEADS = 12
SEG_ROW = 8
AXES = ("tower", "dp")
HOPS = ((8, 2, 4, 1), (1, 8, 2, 4))
POOL_HOPS = ((1, 4, 2), (4, 2, 1))

loss_scale = 65536.0
f32 = jnp.float32
bf16 = jnp.bfloat16
LIMIT = 56 << 20


def call_params():
    return pltpu.CompilerParams(vmem_limit_bytes=LIMIT)


def hop_pairs(dp_size, flip):
    result = []
    for device in range(2 * dp_size):
        tower, place = divmod(device, dp_size)
        tower_bit, place_bits = flip(place & 1)
        result.append((device, (tower ^ tower_bit) * dp_size + (place ^ place_bits)))
    return result


def swap_hop(value, dp_size, masks):
    pairs = hop_pairs(dp_size, lambda core: (masks[core] >> 3, (masks[core] & 7) << 1))
    return lax.ppermute(value, AXES, pairs)


def swap_core(value, dp_size):
    return lax.ppermute(value, AXES, hop_pairs(dp_size, lambda core: (0, 1)))


def swap_place(value, dp_size, bits):
    return lax.ppermute(value, AXES, hop_pairs(dp_size, lambda core: (0, bits)))


def span(masks):
    result = [0]
    for mask in reversed(masks):
        result = result + [mask ^ entry for entry in result]
    return result


def place_tables(dp_size):
    tower = lax.axis_index("tower")
    place = lax.axis_index("dp")
    core = place & 1
    unit = (tower << 3) | ((place >> 1) & 7)
    lists = []
    for hops in HOPS:
        order = span(hops)
        lists.append([order.index(mask) for mask in range(16)])
    inverse = jnp.array(lists, jnp.int32)
    rows = inverse[:, unit ^ jnp.arange(16, dtype=jnp.int32)]
    return core, jnp.where(core == 0, rows, rows[::-1])


def grad_blocks(lhs, rhs, core, table, extra=None, smalls=()):
    count, rows = lhs.shape
    half = rhs.shape[1] // 2
    half_extra = extra[1].shape[1] // 2 if extra else 0
    tile = half // 3
    block = rows // 16
    total = half + half_extra + (128 if smalls else 0)
    per_block = -(-sum(entry.shape[1] for entry, _ in smalls) // (32 * 128))
    meta = jnp.concatenate([core[None], table.reshape(32)])

    def body(meta_ref, lhs_ref, rhs_ref, *refs):
        refs = list(refs)
        turned_ref = refs.pop()
        kept_ref = refs.pop()
        sent_ref = refs.pop()
        step = pl.program_id(0)
        on_zero = meta_ref[0] == 0

        @pl.when(step == 0)
        def _():
            turned_ref[...] = lhs_ref[...].T

        part = dot(turned_ref[...], rhs_ref[...])

        @pl.when(step < 3)
        def _():
            at = pl.multiple_of(step * tile, 128)
            for number in range(16):
                sent_ref[meta_ref[17 + number], :, pl.ds(at, tile)] = part[
                    number * block : (number + 1) * block
                ].astype(bf16)

        @pl.when(step >= 3)
        def _():
            at = pl.multiple_of((step - 3) * tile, 128)
            for number in range(16):
                kept_ref[meta_ref[1 + number], :, pl.ds(at, tile)] = part[
                    number * block : (number + 1) * block
                ]

        @pl.when(step == 5)
        def _():
            at = half
            if extra:
                more = dot(refs[0][...], refs[1][...], 0, 0)
                left, right = more[:, :half_extra], more[:, half_extra:]
                kept = jnp.where(on_zero, left, right)
                sent = jnp.where(on_zero, right, left).astype(bf16)
                for number in range(16):
                    lines = slice(number * block, (number + 1) * block)
                    sent_ref[meta_ref[17 + number], :, at : at + half_extra] = sent[lines]
                    kept_ref[meta_ref[1 + number], :, at : at + half_extra] = kept[lines]
                at += half_extra
            if smalls:
                lines = []
                for (entry, row), ref in zip(smalls, refs[2 if extra else 0 :]):
                    for start in range(0, entry.shape[1], 128):
                        lines.append(ref[row : row + 1, start : start + 128])
                lines += [jnp.zeros((1, 128), f32)] * (32 * per_block - len(lines))
                fill = jnp.zeros((block - per_block, 128), f32)
                for number in range(16):
                    first = number * per_block
                    second = (16 + number) * per_block
                    left = jnp.concatenate(lines[first : first + per_block] + [fill], 0)
                    right = jnp.concatenate(lines[second : second + per_block] + [fill], 0)
                    sent_ref[meta_ref[17 + number], :, at:] = jnp.where(
                        on_zero, right, left
                    ).astype(bf16)
                    kept_ref[meta_ref[1 + number], :, at:] = jnp.where(on_zero, left, right)

    def column(step, meta_ref):
        side = jnp.where(step < 3, 1 - meta_ref[0], meta_ref[0])
        return (0, side * 3 + lax.rem(step, 3))

    operands = [lhs, rhs] + list(extra or ()) + [entry for entry, _ in smalls]
    in_specs = [
        pl.BlockSpec(lhs.shape, lambda step, meta_ref: (0, 0), pipeline_mode=pl.Buffered(1)),
        pl.BlockSpec((count, tile), column),
    ] + [
        pl.BlockSpec(entry.shape, lambda step, meta_ref: (0, 0), pipeline_mode=pl.Buffered(1))
        for entry in operands[2:]
    ]
    return pl.pallas_call(
        body,
        out_shape=[
            jax.ShapeDtypeStruct((16, block, total), bf16),
            jax.ShapeDtypeStruct((16, block, total), f32),
        ],
        grid_spec=pltpu.PrefetchScalarGridSpec(
            num_scalar_prefetch=1,
            grid=(6,),
            in_specs=in_specs,
            out_specs=[
                pl.BlockSpec((16, block, total), lambda step, meta_ref: (0, 0, 0))
                for _ in range(2)
            ],
            scratch_shapes=[pltpu.VMEM((rows, count), bf16)],
        ),
        compiler_params=call_params(),
        cost_estimate=pl.CostEstimate(
            flops=4 * count * rows * (half + half_extra),
            bytes_accessed=2 * count * (rows + 2 * half) + 6 * rows * total,
            transcendentals=0,
        ),
    )(meta, *operands)


def finish(mine, theirs, core, table, widths, small_widths=()):
    block = mine.shape[1]
    rows = 16 * block
    tiles = 4
    per_tile = 16 // tiles
    meta = jnp.concatenate([core[None], table.reshape(32)])
    per_block = -(-sum(small_widths) // (32 * 128))

    def body(meta_ref, mine_ref, theirs_ref, *outs):
        step = pl.program_id(0)

        def fill(first_ref, first_at, second_ref, second_at):
            for inner in range(per_tile):
                number = step * per_tile + inner
                first = meta_ref[first_at + number]
                second = meta_ref[second_at + number]
                start = 0
                for out_ref, width in zip(outs, widths):
                    lines = slice(inner * block, (inner + 1) * block)
                    out_ref[lines, :width] = first_ref[first, :, start : start + width].astype(f32)
                    out_ref[lines, width:] = second_ref[second, :, start : start + width].astype(
                        f32
                    )
                    start += width

            @pl.when(step == tiles - 1)
            def _():
                index = 0
                for out_ref, width in zip(outs[len(widths) :], small_widths):
                    for start_at in range(0, width, 128):
                        group, line = divmod(index, per_block)
                        ref, at = (first_ref, first_at) if group < 16 else (second_ref, second_at)
                        spot = meta_ref[at + group % 16]
                        out_ref[:, start_at : start_at + 128] = ref[
                            spot, line : line + 1, sum(widths) :
                        ].astype(f32)
                        index += 1

        @pl.when(meta_ref[0] == 0)
        def _():
            fill(mine_ref, 1, theirs_ref, 17)

        @pl.when(meta_ref[0] != 0)
        def _():
            fill(theirs_ref, 17, mine_ref, 1)

    whole = pl.BlockSpec(mine.shape, lambda step, meta_ref: (0, 0, 0))
    out_shape = [jax.ShapeDtypeStruct((rows, 2 * width), f32) for width in widths]
    out_specs = [
        pl.BlockSpec((rows // tiles, 2 * width), lambda step, meta_ref: (step, 0))
        for width in widths
    ]
    for width in small_widths:
        out_shape.append(jax.ShapeDtypeStruct((1, width), f32))
        out_specs.append(pl.BlockSpec((1, width), lambda step, meta_ref: (0, 0)))
    return pl.pallas_call(
        body,
        out_shape=out_shape,
        grid_spec=pltpu.PrefetchScalarGridSpec(
            num_scalar_prefetch=1, grid=(tiles,), in_specs=[whole, whole], out_specs=out_specs
        ),
        compiler_params=call_params(),
        cost_estimate=pl.CostEstimate(
            flops=0, bytes_accessed=6 * mine.size * 2, transcendentals=0
        ),
    )(meta, mine, theirs)


def sum_over_all(sent, kept, dp_size):
    terms = [kept, swap_core(sent, dp_size)]

    def piece(start, stop):
        return sum(term[start:stop].astype(f32) for term in terms)

    size = 16
    for hop in range(4):
        size //= 2
        part = piece(size, 2 * size).astype(bf16)
        terms.append(swap_hop(part, dp_size, (HOPS[0][hop], HOPS[1][hop])))
    own = piece(0, 1)
    bits = 16
    while bits < dp_size:
        own = own + swap_place(own.astype(bf16), dp_size, bits).astype(f32)
        bits *= 2
    whole = own.astype(bf16)
    for hop in (3, 2, 1, 0):
        whole = jnp.concatenate(
            [whole, swap_hop(whole, dp_size, (HOPS[0][hop], HOPS[1][hop]))], 0
        )
    return whole, swap_core(whole, dp_size)


def gather_pooled(pooled_low, dp_size):
    rows = lax.ppermute(pooled_low, "tower", [(0, 1), (1, 0)])[None]
    extra = []
    bits = 8
    while 2 * bits < dp_size:
        extra.append(bits)
        bits *= 2
    orders = [list(hops) + extra for hops in POOL_HOPS]
    spans = [[0], [0]]
    for first, second in zip(*orders):
        rows = jnp.concatenate(
            [rows, swap_hop(rows, dp_size, (first, second))]
            if max(first, second) < 8
            else [rows, swap_place(rows, dp_size, 2 * first)],
            0,
        )
        spans = [
            entry + [mask ^ old for old in entry] for entry, mask in zip(spans, (first, second))
        ]
    return rows, swap_core(rows, dp_size), spans


def dot(left, right, left_dim=1, right_dim=0, **kwargs):
    return lax.dot_general(
        left,
        right,
        (((left_dim,), (right_dim,)), ((), ())),
        preferred_element_type=f32,
        **kwargs,
    )


def exact_dot(left, right, left_dim=1, right_dim=0):
    return dot(left, right, left_dim, right_dim, precision=lax.Precision.HIGHEST)


def norm_parts(values_in):
    centered = values_in - jnp.mean(values_in, -1, keepdims=True)
    inv_std = lax.rsqrt(jnp.mean(centered * centered, -1, keepdims=True) + 1e-12)
    return centered * inv_std, inv_std


def norm_back(gradient, normed, inv_std, gain_vec):
    scaled = gradient * gain_vec
    inner = (
        scaled
        - jnp.mean(scaled, -1, keepdims=True)
        - normed * jnp.mean(scaled * normed, -1, keepdims=True)
    )
    return inner * inv_std


ERFC = (
    0.22567586600780487,
    0.22566956281661987,
    0.20784325897693634,
    0.16853809356689453,
    0.14144566655158997,
    -0.0056367916986346245,
    0.16911932826042175,
    -0.1829221397638321,
    0.05026727914810181,
)


def gelu_pair(up):
    bell = jnp.exp2((-0.5 / math.log(2.0)) * (up * up))
    inner = 1.0 / (1.0 + (0.4 / math.sqrt(2.0)) * jnp.abs(up))
    series = jnp.full_like(up, 0.5 * ERFC[-1])
    for factor in ERFC[-2::-1]:
        series = series * inner + 0.5 * factor
    tail = series * inner * bell
    below = jnp.where(up < 0.0, tail, 1.0 - tail)
    return up * below, below + (up * bell) * (1.0 / math.sqrt(2.0 * math.pi))


def row_spec(shape):
    return pl.BlockSpec(shape, lambda step: (step,) + (0,) * (len(shape) - 1))


def full_spec(array):
    rank = len(array.shape)
    return pl.BlockSpec(array.shape, lambda step: (0,) * rank, pipeline_mode=pl.Buffered(1))


def same_sentence(seg_row):
    length = seg_row.shape[1]
    across = jnp.broadcast_to(seg_row.astype(f32), (length, length))
    return across == across.T


def sentence_onehot(seg_refs, rows):
    length = seg_refs[0].shape[1]
    parts = []
    for row in range(rows):
        numbers = lax.broadcasted_iota(jnp.int32, (SEG_ROW, length), 0)
        hit = (numbers == seg_refs[row]).astype(f32)
        empty = jnp.zeros((SEG_ROW, length), f32)
        parts.append(jnp.concatenate([empty] * row + [hit] + [empty] * (rows - 1 - row), 1))
    return jnp.concatenate(parts, 0)


def attention_kernel(tokens, seg_rows, w_qkv, b_query, b_value, w_out, b_out):
    count, width = tokens.shape
    rows_all, length = seg_rows.shape[0], seg_rows.shape[2]
    rows = math.gcd(2, rows_all)
    tile = rows * length
    head_dim = width // HEADS
    scale = 1.0 / math.sqrt(head_dim)

    def body(tok_ref, seg_ref, wqkv_ref, bq_ref, bv_ref, wout_ref, bout_ref, *outs):
        qkv_ref, ctx_ref, sum_ref = outs
        tok = tok_ref[...]
        qkv_ref[:, :width] = (dot(tok, wqkv_ref[:, :width]) + bq_ref[...]).astype(bf16)
        qkv_ref[:, width : 2 * width] = dot(tok, wqkv_ref[:, width : 2 * width]).astype(bf16)
        qkv_ref[:, 2 * width :] = (dot(tok, wqkv_ref[:, 2 * width :]) + bv_ref[...]).astype(bf16)
        first = lax.broadcasted_iota(jnp.int32, (length, 2 * head_dim), 1) < head_dim
        zero = jnp.zeros((length, 2 * head_dim), bf16)
        for row in range(rows):
            lines = slice(row * length, (row + 1) * length)
            mask = same_sentence(seg_ref[row])
            mask = jnp.concatenate([mask, mask], 0)
            for pair in range(HEADS // 2):
                at = pair * 2 * head_dim
                query = qkv_ref[lines, at : at + 2 * head_dim]
                key = qkv_ref[lines, width + at : width + at + 2 * head_dim]
                value = qkv_ref[lines, 2 * width + at : 2 * width + at + 2 * head_dim]
                both = jnp.concatenate(
                    [jnp.where(first, query, zero), jnp.where(first, zero, query)], 0
                )
                score = jnp.where(mask, dot(both, key, 1, 1) * scale, -1e30)
                expo = jnp.exp(score - jnp.max(score, -1, keepdims=True))
                attn = (expo * (1.0 / jnp.sum(expo, -1, keepdims=True))).astype(bf16)
                attn = jnp.concatenate([attn[:length], attn[length:]], 1)
                values = jnp.concatenate(
                    [jnp.where(first, value, zero), jnp.where(first, zero, value)], 0
                )
                ctx_ref[lines, at : at + 2 * head_dim] = dot(attn, values).astype(bf16)
        sum_ref[...] = tok.astype(f32) + (dot(ctx_ref[...], wout_ref[...]) + bout_ref[...])

    operands = [w_qkv, b_query[None], b_value[None], w_out, b_out[None]]
    return pl.pallas_call(
        body,
        out_shape=[
            jax.ShapeDtypeStruct((count, 3 * width), bf16),
            jax.ShapeDtypeStruct((count, width), bf16),
            jax.ShapeDtypeStruct((count, width), f32),
        ],
        grid=(rows_all // rows,),
        in_specs=[row_spec((tile, width)), row_spec((rows, 1, length))]
        + [full_spec(entry) for entry in operands],
        out_specs=[
            row_spec((tile, 3 * width)),
            row_spec((tile, width)),
            row_spec((tile, width)),
        ],
        compiler_params=call_params(),
        cost_estimate=pl.CostEstimate(
            flops=2 * count * width * (4 * width + 2 * length),
            bytes_accessed=16 * count * width,
            transcendentals=count * HEADS * length,
        ),
    )(tokens, seg_rows, *operands)


def forward_kernel(first_sum, seg_rows, gain_one, shift_one, w_in, b_in, w_down, b_down, gain_two, shift_two):
    count, width = first_sum.shape
    rows_all, length = seg_rows.shape[0], seg_rows.shape[2]
    rows = math.gcd(2, rows_all)
    tile = rows * length
    ff_width = w_in.shape[1]
    chunk = 256

    def body(x_ref, seg_ref, g1_ref, s1_ref, win_ref, bin_ref, wdown_ref, bdown_ref, g2_ref, s2_ref, *outs):
        low_ref, act_ref, slope_ref, sum_ref, out_ref, pool_ref = outs
        normed, _ = norm_parts(x_ref[...])
        hidden = normed * g1_ref[...] + s1_ref[...]
        low = hidden.astype(bf16)
        low_ref[...] = low
        total = hidden + bdown_ref[...]
        for start in range(0, ff_width, chunk):
            part = slice(start, start + chunk)
            value, slope = gelu_pair(dot(low, win_ref[:, part]) + bin_ref[:, part])
            act = value.astype(bf16)
            act_ref[:, part] = act
            slope_ref[:, part] = slope.astype(bf16)
            total = total + dot(act, wdown_ref[part, :])
        sum_ref[...] = total
        normed, _ = norm_parts(total)
        result = normed * g2_ref[...] + s2_ref[...]
        out_ref[...] = result.astype(bf16)
        onehot = sentence_onehot([seg_ref[row] for row in range(rows)], rows)
        pool_ref[...] = (
            exact_dot(onehot, result) / jnp.sum(onehot, -1, keepdims=True)
        ).astype(bf16)

    operands = [
        gain_one[None],
        shift_one[None],
        w_in,
        b_in[None],
        w_down,
        b_down[None],
        gain_two[None],
        shift_two[None],
    ]
    return pl.pallas_call(
        body,
        out_shape=[
            jax.ShapeDtypeStruct((count, width), bf16),
            jax.ShapeDtypeStruct((count, ff_width), bf16),
            jax.ShapeDtypeStruct((count, ff_width), bf16),
            jax.ShapeDtypeStruct((count, width), f32),
            jax.ShapeDtypeStruct((count, width), bf16),
            jax.ShapeDtypeStruct((rows_all * SEG_ROW, width), bf16),
        ],
        grid=(rows_all // rows,),
        in_specs=[row_spec((tile, width)), row_spec((rows, 1, length))]
        + [full_spec(entry) for entry in operands],
        out_specs=[
            row_spec((tile, width)),
            row_spec((tile, ff_width)),
            row_spec((tile, ff_width)),
            row_spec((tile, width)),
            row_spec((tile, width)),
            row_spec((rows * SEG_ROW, width)),
        ],
        compiler_params=call_params(),
        cost_estimate=pl.CostEstimate(
            flops=4 * count * width * ff_width + 40 * count * ff_width,
            bytes_accessed=4 * count * ff_width + 12 * count * width + 4 * width * ff_width,
            transcendentals=2 * count * ff_width,
        ),
    )(first_sum, seg_rows, *operands)


def loss_kernel(meta, pairs, scores, mine, theirs, pooled_low, seg_rows, second_sum, gain_two, spans):
    count, width = second_sum.shape
    rows_all, length = seg_rows.shape[0], seg_rows.shape[2]
    rows = math.gcd(2, rows_all)
    tile = rows * length
    sentences = rows * SEG_ROW
    slots = pooled_low.shape[0]
    pair_count = pairs.shape[0] * 128
    per_row = 128 // slots
    groups = rows_all // rows

    def body(
        meta_ref, pairs_ref, scores_ref, mine_ref, theirs_ref, pool_ref, seg_ref, x_ref, g2_ref, *rest
    ):
        mid_ref, low_ref, grads_ref, other_ref, target_ref = rest
        step = pl.program_id(0)

        @pl.when(step == 0)
        def _():
            grads_ref[...] = jnp.zeros_like(grads_ref)
            place = meta_ref[1]
            on_first = meta_ref[0] == 0
            core = place & 1
            lane = lax.broadcasted_iota(jnp.int32, (1, 128), 1)

            def own_column(ref):
                line = ref[pl.ds(place // per_row, 1), :].astype(f32)
                column = jnp.broadcast_to(line, (128, 128)).T
                result = column[:slots]
                for part in range(1, per_row):
                    result = jnp.where(
                        place % per_row == part, column[part * slots : (part + 1) * slots], result
                    )
                return result

            ids = (lax.broadcasted_iota(jnp.int32, (slots, 128), 0) + place * slots).astype(f32)
            wanted = jnp.where(on_first, own_column(pairs_ref), ids)
            target = jnp.where(on_first, own_column(scores_ref), jnp.zeros((slots, 128), f32))
            other = jnp.zeros((slots, width), f32)
            gathered = jnp.zeros((slots, 128), f32)
            for side, ref in enumerate((mine_ref, theirs_ref)):
                for spot in range(len(spans[0])):
                    here = place ^ side ^ (jnp.where(core == side, spans[0][spot], spans[1][spot]) << 1)
                    line = here // per_row
                    offered = jnp.where(
                        on_first,
                        (line * 128 + lane).astype(f32),
                        pairs_ref[pl.ds(line, 1), :].astype(f32),
                    )
                    inside = (lane // slots) == here % per_row
                    hit = jnp.logical_and(wanted == offered, inside)
                    block = ref[spot]
                    other = other + dot(
                        hit.astype(f32).astype(bf16), jnp.concatenate([block] * per_row, 0)
                    )
                    gathered = gathered + jnp.where(hit, scores_ref[pl.ds(line, 1), :], 0.0)
            gathered = jnp.broadcast_to(jnp.sum(gathered, -1, keepdims=True), (slots, 128))
            target = jnp.where(on_first, target, gathered)
            for group in range(groups):
                part = slice(group * sentences, (group + 1) * sentences)
                other_ref[group] = other[part]
                target_ref[group] = target[part]

        mine = pool_ref[...].astype(f32)
        other = other_ref[step]
        inv_mine = lax.rsqrt(jnp.sum(mine * mine, -1, keepdims=True) + 1e-06)
        inv_other = lax.rsqrt(jnp.sum(other * other, -1, keepdims=True) + 1e-06)
        cosine = jnp.sum(mine * other, -1, keepdims=True) * inv_mine * inv_other
        coeff = loss_scale * 2.0 * (cosine - target_ref[step][:, :1]) / pair_count
        d_pooled = coeff * (
            other * (inv_mine * inv_other) - (cosine * inv_mine * inv_mine) * mine
        )
        onehot = sentence_onehot([seg_ref[row] for row in range(rows)], rows)
        per_token = d_pooled / jnp.sum(onehot, -1, keepdims=True)
        d_output = exact_dot(onehot, per_token, 0, 0)
        normed, inv_std = norm_parts(x_ref[...])
        d_mid = norm_back(d_output, normed, inv_std, g2_ref[...])
        mid_ref[...] = d_mid
        low_ref[...] = d_mid.astype(bf16)
        grads_ref[0:1] += jnp.sum(d_output * normed, 0, keepdims=True)
        grads_ref[1:2] += jnp.sum(d_output, 0, keepdims=True)
        grads_ref[2:3] += jnp.sum(d_mid, 0, keepdims=True)

    return pl.pallas_call(
        body,
        out_shape=[
            jax.ShapeDtypeStruct((count, width), f32),
            jax.ShapeDtypeStruct((count, width), bf16),
            jax.ShapeDtypeStruct((8, width), f32),
        ],
        grid=(groups,),
        in_specs=[
            pl.BlockSpec(memory_space=pltpu.SMEM),
            full_spec(pairs),
            full_spec(scores),
            full_spec(mine),
            full_spec(theirs),
            row_spec((sentences, width)),
            row_spec((rows, 1, length)),
            row_spec((tile, width)),
            full_spec(gain_two[None]),
        ],
        out_specs=[
            row_spec((tile, width)),
            row_spec((tile, width)),
            pl.BlockSpec((8, width), lambda step: (0, 0)),
        ],
        scratch_shapes=[
            pltpu.VMEM((groups, sentences, width), f32),
            pltpu.VMEM((groups, sentences, 128), f32),
        ],
        compiler_params=call_params(),
        cost_estimate=pl.CostEstimate(
            flops=100 * count * width, bytes_accessed=10 * count * width, transcendentals=count
        ),
    )(meta, pairs, scores, mine, theirs, pooled_low, seg_rows, second_sum, gain_two[None])


def backward_kernel(d_mid, slope, first_sum, gain_one, w_in, w_down, w_out):
    count, width = first_sum.shape
    ff_width = w_in.shape[1]
    tile = math.gcd(count, 256)
    chunk = 512

    def body(mid_ref, slope_ref, x_ref, g1_ref, win_ref, wdown_ref, wout_ref, *outs):
        up_ref, first_ref, low_ref, ctx_ref, wide_ref, grads_ref = outs

        @pl.when(pl.program_id(0) == 0)
        def _():
            grads_ref[...] = jnp.zeros_like(grads_ref)
            wide_ref[...] = jnp.zeros_like(wide_ref)

        d_hidden = mid_ref[...]
        mid_low = d_hidden.astype(bf16)
        for start in range(0, ff_width, chunk):
            part = slice(start, start + chunk)
            d_up = dot(mid_low, wdown_ref[part, :], 1, 1) * slope_ref[:, part].astype(f32)
            wide_ref[0:1, part] += jnp.sum(d_up, 0, keepdims=True)
            up_low = d_up.astype(bf16)
            up_ref[:, part] = up_low
            d_hidden = d_hidden + dot(up_low, win_ref[:, part], 1, 1)
        normed, inv_std = norm_parts(x_ref[...])
        d_first = norm_back(d_hidden, normed, inv_std, g1_ref[...])
        first_ref[...] = d_first
        first_low = d_first.astype(bf16)
        low_ref[...] = first_low
        ctx_ref[...] = dot(first_low, wout_ref[...], 1, 1).astype(bf16)
        grads_ref[0:1] += jnp.sum(d_first, 0, keepdims=True)
        grads_ref[1:2] += jnp.sum(d_hidden * normed, 0, keepdims=True)
        grads_ref[2:3] += jnp.sum(d_hidden, 0, keepdims=True)

    operands = [gain_one[None], w_in, w_down, w_out]
    return pl.pallas_call(
        body,
        out_shape=[
            jax.ShapeDtypeStruct((count, ff_width), bf16),
            jax.ShapeDtypeStruct((count, width), f32),
            jax.ShapeDtypeStruct((count, width), bf16),
            jax.ShapeDtypeStruct((count, width), bf16),
            jax.ShapeDtypeStruct((8, ff_width), f32),
            jax.ShapeDtypeStruct((8, width), f32),
        ],
        grid=(count // tile,),
        in_specs=[row_spec((tile, width)), row_spec((tile, ff_width)), row_spec((tile, width))]
        + [full_spec(entry) for entry in operands],
        out_specs=[
            row_spec((tile, ff_width)),
            row_spec((tile, width)),
            row_spec((tile, width)),
            row_spec((tile, width)),
            pl.BlockSpec((8, ff_width), lambda step: (0, 0)),
            pl.BlockSpec((8, width), lambda step: (0, 0)),
        ],
        compiler_params=call_params(),
        cost_estimate=pl.CostEstimate(
            flops=4 * count * width * ff_width + 2 * count * width * width,
            bytes_accessed=4 * count * ff_width + 16 * count * width + 4 * width * ff_width,
            transcendentals=0,
        ),
    )(d_mid, slope, first_sum, *operands)


def attention_back_kernel(qkv, d_context, seg_rows):
    count, width = d_context.shape
    rows_all, length = seg_rows.shape[0], seg_rows.shape[2]
    rows = math.gcd(2, rows_all)
    tile = rows * length
    head_dim = width // HEADS
    scale = 1.0 / math.sqrt(head_dim)

    def body(qkv_ref, dctx_ref, seg_ref, joint_ref, grads_ref):
        @pl.when(pl.program_id(0) == 0)
        def _():
            grads_ref[...] = jnp.zeros_like(grads_ref)

        first = lax.broadcasted_iota(jnp.int32, (length, 2 * head_dim), 1) < head_dim
        zero = jnp.zeros((length, 2 * head_dim), bf16)

        def split(part):
            return jnp.concatenate([jnp.where(first, part, zero), jnp.where(first, zero, part)], 0)

        def beside(part):
            return jnp.concatenate([part[:length], part[length:]], 1)

        for row in range(rows):
            lines = slice(row * length, (row + 1) * length)
            mask = same_sentence(seg_ref[row])
            mask = jnp.concatenate([mask, mask], 0)
            for pair in range(HEADS // 2):
                at = pair * 2 * head_dim
                here = slice(at, at + 2 * head_dim)
                key_here = slice(width + at, width + at + 2 * head_dim)
                value_here = slice(2 * width + at, 2 * width + at + 2 * head_dim)
                query = split(qkv_ref[lines, here])
                key = qkv_ref[lines, key_here]
                grad = split(dctx_ref[lines, here])
                score = jnp.where(mask, dot(query, key, 1, 1) * scale, -1e30)
                expo = jnp.exp(score - jnp.max(score, -1, keepdims=True))
                attn = expo * (1.0 / jnp.sum(expo, -1, keepdims=True))
                d_attn = dot(grad, qkv_ref[lines, value_here], 1, 1)
                weighted = attn * d_attn
                d_score = weighted - attn * jnp.sum(weighted, -1, keepdims=True)
                d_score = d_score.astype(bf16)
                d_value = dot(attn.astype(bf16), grad, 0, 0)
                d_key = dot(d_score, query, 0, 0) * scale
                d_query = dot(beside(d_score), split(key)) * scale
                joint_ref[lines, here] = d_query.astype(bf16)
                joint_ref[lines, key_here] = d_key.astype(bf16)
                joint_ref[lines, value_here] = d_value.astype(bf16)
                grads_ref[0:1, here] += jnp.sum(d_query, 0, keepdims=True)
                grads_ref[1:2, here] += jnp.sum(d_value, 0, keepdims=True)

    return pl.pallas_call(
        body,
        out_shape=[
            jax.ShapeDtypeStruct((count, 3 * width), bf16),
            jax.ShapeDtypeStruct((8, width), f32),
        ],
        grid=(rows_all // rows,),
        in_specs=[
            row_spec((tile, 3 * width)),
            row_spec((tile, width)),
            row_spec((rows, 1, length)),
        ],
        out_specs=[row_spec((tile, 3 * width)), pl.BlockSpec((8, width), lambda step: (0, 0))],
        compiler_params=call_params(),
        cost_estimate=pl.CostEstimate(
            flops=14 * count * width * length,
            bytes_accessed=14 * count * width,
            transcendentals=count * HEADS * length,
        ),
    )(qkv, d_context, seg_rows)


def on_device(
    tokens,
    segments,
    pairs,
    scores,
    w_qkv,
    b_query,
    b_value,
    w_out,
    b_out,
    gain_one,
    shift_one,
    w_in,
    b_in,
    w_down,
    b_down,
    gain_two,
    shift_two,
):
    dp_size = lax.axis_size("dp")
    core, table = place_tables(dp_size)
    place = jnp.stack([lax.axis_index("tower"), lax.axis_index("dp")]).astype(jnp.int32)
    flat_rows = tokens[0]
    seg_rows = segments[0][:, None, :]
    width = flat_rows.shape[1]
    ff_width = w_in.shape[1]
    qkv, context, first_sum = attention_kernel(
        flat_rows, seg_rows, w_qkv, b_query, b_value, w_out, b_out
    )
    hidden_low, act, slope, second_sum, output_rows, pooled_low = forward_kernel(
        first_sum, seg_rows, gain_one, shift_one, w_in, b_in, w_down, b_down, gain_two, shift_two
    )
    mine, theirs, spans = gather_pooled(pooled_low, dp_size)
    d_mid, d_mid_low, grads_two = loss_kernel(
        place,
        pairs.reshape(-1, 128),
        scores.reshape(-1, 128),
        mine,
        theirs,
        pooled_low,
        seg_rows,
        second_sum,
        gain_two,
        spans,
    )
    grad_w_down = jnp.einsum("nf,nd->fd", act, d_mid_low, preferred_element_type=f32)
    grad_w_down = lax.psum(grad_w_down.astype(bf16), AXES)
    d_up_low, d_first, d_first_low, d_context, grads_wide, grads_one = backward_kernel(
        d_mid, slope, first_sum, gain_one, w_in, w_down, w_out
    )
    in_sum = sum_over_all(
        *grad_blocks(hidden_low, d_up_low, core, table, (context, d_first_low)), dp_size
    )
    d_joint, grads_attn = attention_back_kernel(qkv, d_context, seg_rows)
    qkv_sum = sum_over_all(
        *grad_blocks(
            flat_rows,
            d_joint,
            core,
            table,
            None,
            [
                (grads_attn, 0),
                (grads_attn, 1),
                (grads_one, 0),
                (grads_one, 1),
                (grads_one, 2),
                (grads_wide, 0),
                (grads_two, 2),
                (grads_two, 0),
                (grads_two, 1),
            ],
        ),
        dp_size,
    )
    grad_tokens = d_first + jnp.einsum("ne,de->nd", d_joint, w_qkv, preferred_element_type=f32)
    grad_w_in, grad_w_out = finish(*in_sum, core, table, [ff_width // 2, width // 2])
    small_widths = [width] * 5 + [ff_width] + [width] * 3
    grad_w_qkv, *smalls = finish(*qkv_sum, core, table, [3 * width // 2], small_widths)
    smalls = [entry.reshape(-1) for entry in smalls]
    return (
        output_rows[None],
        grad_tokens[None],
        grad_w_qkv,
        smalls[0],
        smalls[1],
        grad_w_out,
        smalls[2],
        smalls[3],
        smalls[4],
        grad_w_in,
        smalls[5],
        grad_w_down.astype(f32),
        smalls[6],
        smalls[7],
        smalls[8],
    )


def solution(mesh):
    return jax.shard_map(
        on_device,
        mesh=mesh,
        in_specs=(
            P("tower", "dp", None),
            P("tower", "dp", None),
            P(),
            P(),
            P(),
            P(),
            P(),
            P(),
            P(),
            P(),
            P(),
            P(),
            P(),
            P(),
            P(),
            P(),
            P(),
        ),
        out_specs=(
            P("tower", "dp", None),
            P("tower", "dp", None),
            P(),
            P(),
            P(),
            P(),
            P(),
            P(),
            P(),
            P(),
            P(),
            P(),
            P(),
            P(),
            P(),
        ),
        check_vma=False,
    )
```

```python
import math
from functools import partial

import jax
import jax.numpy as jnp
from jax import lax
from jax.experimental import pallas as pl
from jax.experimental.pallas import tpu as pltpu
from jax.sharding import PartitionSpec as P

HEADS = 12
SEG_ROW = 8
AXES = ("tower", "dp")
HOPS = ((8, 2, 4, 1), (1, 8, 2, 4))
POOL_HOPS = ((1, 4, 2), (4, 2, 1))

loss_scale = 65536.0
f32 = jnp.float32
bf16 = jnp.bfloat16
LIMIT = 56 << 20


def call_params():
    return pltpu.CompilerParams(vmem_limit_bytes=LIMIT)


def hop_pairs(dp_size, flip):
    result = []
    for device in range(2 * dp_size):
        tower, place = divmod(device, dp_size)
        tower_bit, place_bits = flip(place & 1)
        result.append((device, (tower ^ tower_bit) * dp_size + (place ^ place_bits)))
    return result


def swap_hop(value, dp_size, masks):
    pairs = hop_pairs(dp_size, lambda core: (masks[core] >> 3, (masks[core] & 7) << 1))
    return lax.ppermute(value, AXES, pairs)


def swap_core(value, dp_size):
    return lax.ppermute(value, AXES, hop_pairs(dp_size, lambda core: (0, 1)))


def swap_place(value, dp_size, bits):
    return lax.ppermute(value, AXES, hop_pairs(dp_size, lambda core: (0, bits)))


def span(masks):
    result = [0]
    for mask in reversed(masks):
        result = result + [mask ^ entry for entry in result]
    return result


def place_tables(dp_size):
    tower = lax.axis_index("tower")
    place = lax.axis_index("dp")
    core = place & 1
    unit = (tower << 3) | ((place >> 1) & 7)
    lists = []
    for hops in HOPS:
        order = span(hops)
        lists.append([order.index(mask) for mask in range(16)])
    inverse = jnp.array(lists, jnp.int32)
    rows = inverse[:, unit ^ jnp.arange(16, dtype=jnp.int32)]
    return core, jnp.where(core == 0, rows, rows[::-1])


def grad_half(turned, rhs, half, table, kind, extra=None, smalls=()):
    rows, count = turned.shape
    width = rhs.shape[1] // 2
    tile = 384
    steps = width // tile
    more = extra[1].shape[1] // (2 * tile) if extra else 0
    block = rows // 16
    total = (steps + more) * tile + (128 if smalls else 0)
    per_block = -(-sum(entry.shape[1] for entry, _ in smalls) // (32 * 128))
    meta = jnp.concatenate([half[None], table])

    def body(meta_ref, turned_ref, rhs_ref, *refs):
        out_ref = refs[-1]
        step = pl.program_id(0)

        def store(part, at):
            for number in range(16):
                lines = slice(number * block, (number + 1) * block)
                out_ref[meta_ref[1 + number], :, at] = part[lines].astype(kind)

        def main():
            at = pl.ds(pl.multiple_of(step * tile, 128), tile) if smalls else slice(None)
            store(dot(turned_ref[...], rhs_ref[...]), at)

        if more:
            pl.when(step < steps)(main)

            @pl.when(step >= steps)
            def _():
                store(dot(refs[0][...], refs[1][...]), slice(None))

        else:
            main()
        if smalls:

            @pl.when(step == steps - 1)
            def _():
                lines = []
                for (entry, row), ref in zip(smalls, refs):
                    for start in range(0, entry.shape[1], 128):
                        lines.append(ref[row : row + 1, start : start + 128])
                lines += [jnp.zeros((1, 128), f32)] * (32 * per_block - len(lines))
                fill = jnp.zeros((block - per_block, 128), f32)
                for number in range(16):
                    first = number * per_block
                    second = (16 + number) * per_block
                    left = jnp.concatenate(lines[first : first + per_block], 0)
                    right = jnp.concatenate(lines[second : second + per_block], 0)
                    own = jnp.where(meta_ref[0] == 0, left, right)
                    out_ref[meta_ref[1 + number], :, total - 128 :] = jnp.concatenate(
                        [own, fill], 0
                    ).astype(kind)

    def whole(array):
        return pl.BlockSpec(
            array.shape, lambda step, meta_ref: (0, 0), pipeline_mode=pl.Buffered(1)
        )

    in_specs = [
        whole(turned),
        pl.BlockSpec(
            (count, tile),
            lambda step, meta_ref: (0, meta_ref[0] * steps + jnp.minimum(step, steps - 1)),
        ),
    ]
    operands = [turned, rhs]
    if extra:
        in_specs += [
            whole(extra[0]),
            pl.BlockSpec(
                (count, tile),
                lambda step, meta_ref: (0, meta_ref[0] * more + jnp.maximum(step - steps, 0)),
            ),
        ]
        operands += list(extra)
    in_specs += [whole(entry) for entry, _ in smalls]
    operands += [entry for entry, _ in smalls]
    return pl.pallas_call(
        body,
        out_shape=jax.ShapeDtypeStruct((16, block, total), kind),
        grid_spec=pltpu.PrefetchScalarGridSpec(
            num_scalar_prefetch=1,
            grid=(steps + more,),
            in_specs=in_specs,
            out_specs=pl.BlockSpec((16, block, total), lambda step, meta_ref: (0, 0, 0))
            if smalls
            else pl.BlockSpec((16, block, tile), lambda step, meta_ref: (0, 0, step)),
        ),
        compiler_params=call_params(),
        cost_estimate=pl.CostEstimate(
            flops=2 * count * rows * total,
            bytes_accessed=2 * count * (rows + total) + 3 * rows * total,
            transcendentals=0,
        ),
    )(meta, *operands)


def finish(mine, theirs, core, table, widths, small_widths=()):
    block = mine.shape[1]
    rows = 16 * block
    tiles = 4
    per_tile = 16 // tiles
    meta = jnp.concatenate([core[None], table.reshape(32)])
    per_block = -(-sum(small_widths) // (32 * 128))

    def body(meta_ref, mine_ref, theirs_ref, *outs):
        step = pl.program_id(0)

        def fill(first_ref, first_at, second_ref, second_at):
            for inner in range(per_tile):
                number = step * per_tile + inner
                first = meta_ref[first_at + number]
                second = meta_ref[second_at + number]
                start = 0
                for out_ref, width in zip(outs, widths):
                    lines = slice(inner * block, (inner + 1) * block)
                    out_ref[lines, :width] = first_ref[first, :, start : start + width].astype(f32)
                    out_ref[lines, width:] = second_ref[second, :, start : start + width].astype(
                        f32
                    )
                    start += width

            @pl.when(step == tiles - 1)
            def _():
                index = 0
                for out_ref, width in zip(outs[len(widths) :], small_widths):
                    for start_at in range(0, width, 128):
                        group, line = divmod(index, per_block)
                        ref, at = (first_ref, first_at) if group < 16 else (second_ref, second_at)
                        spot = meta_ref[at + group % 16]
                        values = ref[spot, line : line + 1, sum(widths) :].astype(f32)
                        out_ref[start_at : start_at + 128] = values.reshape(128)
                        index += 1

        @pl.when(meta_ref[0] == 0)
        def _():
            fill(mine_ref, 1, theirs_ref, 17)

        @pl.when(meta_ref[0] != 0)
        def _():
            fill(theirs_ref, 17, mine_ref, 1)

    whole = pl.BlockSpec(mine.shape, lambda step, meta_ref: (0, 0, 0))
    out_shape = [jax.ShapeDtypeStruct((rows, 2 * width), f32) for width in widths]
    out_specs = [
        pl.BlockSpec((rows // tiles, 2 * width), lambda step, meta_ref: (step, 0))
        for width in widths
    ]
    for width in small_widths:
        out_shape.append(jax.ShapeDtypeStruct((width,), f32))
        out_specs.append(pl.BlockSpec((width,), lambda step, meta_ref: (0,)))
    return pl.pallas_call(
        body,
        out_shape=out_shape,
        grid_spec=pltpu.PrefetchScalarGridSpec(
            num_scalar_prefetch=1, grid=(tiles,), in_specs=[whole, whole], out_specs=out_specs
        ),
        compiler_params=call_params(),
        cost_estimate=pl.CostEstimate(
            flops=0, bytes_accessed=6 * mine.size * 2, transcendentals=0
        ),
    )(meta, mine, theirs)


def finish_turned(mine, theirs, core, table):
    block, half = mine.shape[1:]
    tile = 384
    steps = half // tile
    meta = jnp.concatenate([core[None], table.reshape(32)])

    def body(meta_ref, mine_ref, theirs_ref, out_ref):
        own = (pl.program_id(0) // steps) == meta_ref[0]

        def fill(ref, first):
            parts = [ref[meta_ref[first + number]] for number in range(16)]
            out_ref[...] = jnp.concatenate(parts, 0).T.astype(f32)

        @pl.when(own)
        def _():
            fill(mine_ref, 1)

        @pl.when(jnp.logical_not(own))
        def _():
            fill(theirs_ref, 17)

    piece = pl.BlockSpec((16, block, tile), lambda step, meta_ref: (0, 0, lax.rem(step, steps)))
    return pl.pallas_call(
        body,
        out_shape=jax.ShapeDtypeStruct((2 * half, 16 * block), f32),
        grid_spec=pltpu.PrefetchScalarGridSpec(
            num_scalar_prefetch=1,
            grid=(2 * steps,),
            in_specs=[piece, piece],
            out_specs=pl.BlockSpec((tile, 16 * block), lambda step, meta_ref: (step, 0)),
        ),
        compiler_params=call_params(),
        cost_estimate=pl.CostEstimate(
            flops=0, bytes_accessed=12 * mine.size, transcendentals=0
        ),
    )(meta, mine, theirs)


class Sum:
    def __init__(self, sent, dp_size):
        self.dp_size = dp_size
        self.piece = sent
        self.stage = 0
        self.terms = []
        self.whole = None
        self.result = None

    def send(self, piece):
        if self.stage in (0, 9):
            return swap_core(piece, self.dp_size)
        hop = self.stage - 1 if self.stage < 5 else 8 - self.stage
        return swap_hop(piece, self.dp_size, (HOPS[0][hop], HOPS[1][hop]))

    def take(self, received):
        def part(start, stop):
            return sum(term[start:stop].astype(f32) for term in self.terms)

        if self.stage < 5:
            self.terms.append(received)
        if self.stage < 4:
            size = 8 >> self.stage
            self.piece = part(size, 2 * size).astype(bf16)
        elif self.stage == 4:
            own = part(0, 1)
            bits = 16
            while bits < self.dp_size:
                own = own + swap_place(own.astype(bf16), self.dp_size, bits).astype(f32)
                bits *= 2
            self.piece = own.astype(bf16)
        elif self.stage < 9:
            self.piece = jnp.concatenate([self.piece, received], 0)
        else:
            self.result = (self.piece, received)
        self.stage += 1

    def run(self):
        while self.result is None:
            self.take(self.send(self.piece))
        return self.result


def beside(work, entry, *sums, keeps=None):
    entry, pieces = lax.optimization_barrier((entry, [each.piece for each in sums]))
    for each, piece in zip(sums, pieces):
        each.piece = piece
    received = [each.send(each.piece) for each in sums]
    result, received = lax.optimization_barrier((work(entry), received))
    if keeps:
        keeps.terms.append(result)
    for each, value in zip(sums, received):
        each.take(value)
    return result


def gather_pooled(pooled_low, dp_size):
    rows = lax.ppermute(pooled_low, "tower", [(0, 1), (1, 0)])[None]
    extra = []
    bits = 8
    while 2 * bits < dp_size:
        extra.append(bits)
        bits *= 2
    orders = [list(hops) + extra for hops in POOL_HOPS]
    spans = [[0], [0]]
    for first, second in zip(*orders):
        rows = jnp.concatenate(
            [rows, swap_hop(rows, dp_size, (first, second))]
            if max(first, second) < 8
            else [rows, swap_place(rows, dp_size, 2 * first)],
            0,
        )
        spans = [
            entry + [mask ^ old for old in entry] for entry, mask in zip(spans, (first, second))
        ]
    return rows, swap_core(rows, dp_size), spans


def dot(left, right, left_dim=1, right_dim=0, **kwargs):
    return lax.dot_general(
        left,
        right,
        (((left_dim,), (right_dim,)), ((), ())),
        preferred_element_type=f32,
        **kwargs,
    )


def exact_dot(left, right, left_dim=1, right_dim=0):
    return dot(left, right, left_dim, right_dim, precision=lax.Precision.HIGHEST)


def norm_parts(values_in):
    centered = values_in - jnp.mean(values_in, -1, keepdims=True)
    inv_std = lax.rsqrt(jnp.mean(centered * centered, -1, keepdims=True) + 1e-12)
    return centered * inv_std, inv_std


def norm_back(gradient, normed, inv_std, gain_vec):
    scaled = gradient * gain_vec
    inner = (
        scaled
        - jnp.mean(scaled, -1, keepdims=True)
        - normed * jnp.mean(scaled * normed, -1, keepdims=True)
    )
    return inner * inv_std


ERFC = (
    0.22567586600780487,
    0.22566956281661987,
    0.20784325897693634,
    0.16853809356689453,
    0.14144566655158997,
    -0.0056367916986346245,
    0.16911932826042175,
    -0.1829221397638321,
    0.05026727914810181,
)


def gelu_pair(up):
    bell = jnp.exp2((-0.5 / math.log(2.0)) * (up * up))
    inner = 1.0 / (1.0 + (0.4 / math.sqrt(2.0)) * jnp.abs(up))
    series = jnp.full_like(up, 0.5 * ERFC[-1])
    for factor in ERFC[-2::-1]:
        series = series * inner + 0.5 * factor
    tail = series * inner * bell
    below = jnp.where(up < 0.0, tail, 1.0 - tail)
    return up * below, below + (up * bell) * (1.0 / math.sqrt(2.0 * math.pi))


def line(ref, part=slice(None)):
    return ref[part].reshape(1, -1)


def row_spec(shape):
    return pl.BlockSpec(shape, lambda step: (step,) + (0,) * (len(shape) - 1))


def column_spec(shape):
    return pl.BlockSpec(shape, lambda step: (0, step))


def full_spec(array):
    rank = len(array.shape)
    return pl.BlockSpec(array.shape, lambda step: (0,) * rank, pipeline_mode=pl.Buffered(1))


def same_sentence(seg_row):
    length = seg_row.shape[1]
    across = jnp.broadcast_to(seg_row.astype(f32), (length, length))
    return across == across.T


def sentence_onehot(seg_refs, rows):
    length = seg_refs[0].shape[1]
    parts = []
    for row in range(rows):
        numbers = lax.broadcasted_iota(jnp.int32, (SEG_ROW, length), 0)
        hit = (numbers == seg_refs[row]).astype(f32)
        empty = jnp.zeros((SEG_ROW, length), f32)
        parts.append(jnp.concatenate([empty] * row + [hit] + [empty] * (rows - 1 - row), 1))
    return jnp.concatenate(parts, 0)


def attention_kernel(tokens, seg_rows, w_qkv, b_query, b_value, w_out, b_out):
    count, width = tokens.shape
    rows_all, length = seg_rows.shape[0], seg_rows.shape[2]
    rows = math.gcd(2, rows_all)
    tile = rows * length
    head_dim = width // HEADS
    scale = 1.0 / math.sqrt(head_dim)

    def body(tok_ref, seg_ref, wqkv_ref, bq_ref, bv_ref, wout_ref, bout_ref, *outs):
        qkv_ref, turned_ref, tok_turned_ref, sum_ref, ctx_ref = outs
        tok = tok_ref[...]
        tok_turned_ref[...] = tok.T
        qkv_ref[:, :width] = (dot(tok, wqkv_ref[:, :width]) + line(bq_ref)).astype(bf16)
        qkv_ref[:, width : 2 * width] = dot(tok, wqkv_ref[:, width : 2 * width]).astype(bf16)
        qkv_ref[:, 2 * width :] = (dot(tok, wqkv_ref[:, 2 * width :]) + line(bv_ref)).astype(bf16)
        first = lax.broadcasted_iota(jnp.int32, (length, 2 * head_dim), 1) < head_dim
        zero = jnp.zeros((length, 2 * head_dim), bf16)
        for row in range(rows):
            lines = slice(row * length, (row + 1) * length)
            mask = same_sentence(seg_ref[row])
            mask = jnp.concatenate([mask, mask], 0)
            for pair in range(HEADS // 2):
                at = pair * 2 * head_dim
                query = qkv_ref[lines, at : at + 2 * head_dim]
                key = qkv_ref[lines, width + at : width + at + 2 * head_dim]
                value = qkv_ref[lines, 2 * width + at : 2 * width + at + 2 * head_dim]
                both = jnp.concatenate(
                    [jnp.where(first, query, zero), jnp.where(first, zero, query)], 0
                )
                score = jnp.where(mask, dot(both, key, 1, 1) * scale, -1e30)
                expo = jnp.exp(score - jnp.max(score, -1, keepdims=True))
                attn = (expo * (1.0 / jnp.sum(expo, -1, keepdims=True))).astype(bf16)
                attn = jnp.concatenate([attn[:length], attn[length:]], 1)
                values = jnp.concatenate(
                    [jnp.where(first, value, zero), jnp.where(first, zero, value)], 0
                )
                ctx_ref[lines, at : at + 2 * head_dim] = dot(attn, values).astype(bf16)
        context = ctx_ref[...]
        turned_ref[...] = context.T
        sum_ref[...] = tok.astype(f32) + (dot(context, wout_ref[...]) + line(bout_ref))

    operands = [w_qkv, b_query, b_value, w_out, b_out]
    return pl.pallas_call(
        body,
        out_shape=[
            jax.ShapeDtypeStruct((count, 3 * width), bf16),
            jax.ShapeDtypeStruct((width, count), bf16),
            jax.ShapeDtypeStruct((width, count), bf16),
            jax.ShapeDtypeStruct((count, width), f32),
        ],
        grid=(rows_all // rows,),
        in_specs=[row_spec((tile, width)), row_spec((rows, 1, length))]
        + [full_spec(entry) for entry in operands],
        out_specs=[
            row_spec((tile, 3 * width)),
            column_spec((width, tile)),
            column_spec((width, tile)),
            row_spec((tile, width)),
        ],
        scratch_shapes=[pltpu.VMEM((tile, width), bf16)],
        compiler_params=call_params(),
        cost_estimate=pl.CostEstimate(
            flops=2 * count * width * (4 * width + 2 * length),
            bytes_accessed=16 * count * width,
            transcendentals=count * HEADS * length,
        ),
    )(tokens, seg_rows, *operands)


def forward_kernel(first_sum, seg_rows, gain_one, shift_one, w_in, b_in, w_down, b_down, gain_two, shift_two):
    count, width = first_sum.shape
    rows_all, length = seg_rows.shape[0], seg_rows.shape[2]
    rows = math.gcd(2, rows_all)
    tile = rows * length
    ff_width = w_in.shape[1]
    chunk = 256

    def body(x_ref, seg_ref, g1_ref, s1_ref, win_ref, bin_ref, wdown_ref, bdown_ref, g2_ref, s2_ref, *outs):
        low_ref, act_ref, slope_ref, sum_ref, out_ref, pool_ref = outs
        normed, _ = norm_parts(x_ref[...])
        hidden = normed * line(g1_ref) + line(s1_ref)
        low = hidden.astype(bf16)
        low_ref[...] = low.T
        total = hidden + line(bdown_ref)
        for start in range(0, ff_width, chunk):
            part = slice(start, start + chunk)
            value, slope = gelu_pair(dot(low, win_ref[:, part]) + line(bin_ref, part))
            act = value.astype(bf16)
            act_ref[:, part] = act
            slope_ref[:, part] = slope.astype(bf16)
            total = total + dot(act, wdown_ref[part, :])
        sum_ref[...] = total
        normed, _ = norm_parts(total)
        result = normed * line(g2_ref) + line(s2_ref)
        out_ref[...] = result.astype(bf16)
        onehot = sentence_onehot([seg_ref[row] for row in range(rows)], rows)
        pool_ref[...] = (
            exact_dot(onehot, result) / jnp.sum(onehot, -1, keepdims=True)
        ).astype(bf16)

    operands = [
        gain_one,
        shift_one,
        w_in,
        b_in,
        w_down,
        b_down,
        gain_two,
        shift_two,
    ]
    return pl.pallas_call(
        body,
        out_shape=[
            jax.ShapeDtypeStruct((width, count), bf16),
            jax.ShapeDtypeStruct((count, ff_width), bf16),
            jax.ShapeDtypeStruct((count, ff_width), bf16),
            jax.ShapeDtypeStruct((count, width), f32),
            jax.ShapeDtypeStruct((count, width), bf16),
            jax.ShapeDtypeStruct((rows_all * SEG_ROW, width), bf16),
        ],
        grid=(rows_all // rows,),
        in_specs=[row_spec((tile, width)), row_spec((rows, 1, length))]
        + [full_spec(entry) for entry in operands],
        out_specs=[
            column_spec((width, tile)),
            row_spec((tile, ff_width)),
            row_spec((tile, ff_width)),
            row_spec((tile, width)),
            row_spec((tile, width)),
            row_spec((rows * SEG_ROW, width)),
        ],
        compiler_params=call_params(),
        cost_estimate=pl.CostEstimate(
            flops=4 * count * width * ff_width + 40 * count * ff_width,
            bytes_accessed=4 * count * ff_width + 12 * count * width + 4 * width * ff_width,
            transcendentals=2 * count * ff_width,
        ),
    )(first_sum, seg_rows, *operands)


def loss_kernel(meta, pairs, scores, mine, theirs, pooled_low, seg_rows, second_sum, gain_two, spans):
    count, width = second_sum.shape
    rows_all, length = seg_rows.shape[0], seg_rows.shape[2]
    rows = math.gcd(2, rows_all)
    tile = rows * length
    sentences = rows * SEG_ROW
    slots = pooled_low.shape[0]
    pair_count = pairs.shape[0] * 128
    per_row = 128 // slots
    groups = rows_all // rows

    def body(
        meta_ref, pairs_ref, scores_ref, mine_ref, theirs_ref, pool_ref, seg_ref, x_ref, g2_ref, *rest
    ):
        mid_ref, low_ref, grads_ref, other_ref, target_ref = rest
        step = pl.program_id(0)

        @pl.when(step == 0)
        def _():
            grads_ref[...] = jnp.zeros_like(grads_ref)
            place = meta_ref[1]
            on_first = meta_ref[0] == 0
            core = place & 1
            lane = lax.broadcasted_iota(jnp.int32, (1, 128), 1)

            def own_column(ref):
                line = ref[pl.ds(place // per_row, 1), :].astype(f32)
                column = jnp.broadcast_to(line, (128, 128)).T
                result = column[:slots]
                for part in range(1, per_row):
                    result = jnp.where(
                        place % per_row == part, column[part * slots : (part + 1) * slots], result
                    )
                return result

            ids = (lax.broadcasted_iota(jnp.int32, (slots, 128), 0) + place * slots).astype(f32)
            wanted = jnp.where(on_first, own_column(pairs_ref), ids)
            target = jnp.where(on_first, own_column(scores_ref), jnp.zeros((slots, 128), f32))
            other = jnp.zeros((slots, width), f32)
            gathered = jnp.zeros((slots, 128), f32)
            for side, ref in enumerate((mine_ref, theirs_ref)):
                for spot in range(len(spans[0])):
                    here = place ^ side ^ (jnp.where(core == side, spans[0][spot], spans[1][spot]) << 1)
                    line = here // per_row
                    offered = jnp.where(
                        on_first,
                        (line * 128 + lane).astype(f32),
                        pairs_ref[pl.ds(line, 1), :].astype(f32),
                    )
                    inside = (lane // slots) == here % per_row
                    hit = jnp.logical_and(wanted == offered, inside)
                    block = ref[spot]
                    other = other + dot(
                        hit.astype(f32).astype(bf16), jnp.concatenate([block] * per_row, 0)
                    )
                    gathered = gathered + jnp.where(hit, scores_ref[pl.ds(line, 1), :], 0.0)
            gathered = jnp.broadcast_to(jnp.sum(gathered, -1, keepdims=True), (slots, 128))
            target = jnp.where(on_first, target, gathered)
            for group in range(groups):
                part = slice(group * sentences, (group + 1) * sentences)
                other_ref[group] = other[part]
                target_ref[group] = target[part]

        mine = pool_ref[...].astype(f32)
        other = other_ref[step]
        inv_mine = lax.rsqrt(jnp.sum(mine * mine, -1, keepdims=True) + 1e-06)
        inv_other = lax.rsqrt(jnp.sum(other * other, -1, keepdims=True) + 1e-06)
        cosine = jnp.sum(mine * other, -1, keepdims=True) * inv_mine * inv_other
        coeff = loss_scale * 2.0 * (cosine - target_ref[step][:, :1]) / pair_count
        d_pooled = coeff * (
            other * (inv_mine * inv_other) - (cosine * inv_mine * inv_mine) * mine
        )
        onehot = sentence_onehot([seg_ref[row] for row in range(rows)], rows)
        per_token = d_pooled / jnp.sum(onehot, -1, keepdims=True)
        d_output = exact_dot(onehot, per_token, 0, 0)
        normed, inv_std = norm_parts(x_ref[...])
        d_mid = norm_back(d_output, normed, inv_std, line(g2_ref))
        mid_ref[...] = d_mid
        low_ref[...] = d_mid.astype(bf16).T
        grads_ref[0:1] += jnp.sum(d_output * normed, 0, keepdims=True)
        grads_ref[1:2] += jnp.sum(d_output, 0, keepdims=True)
        grads_ref[2:3] += jnp.sum(d_mid, 0, keepdims=True)

    return pl.pallas_call(
        body,
        out_shape=[
            jax.ShapeDtypeStruct((count, width), f32),
            jax.ShapeDtypeStruct((width, count), bf16),
            jax.ShapeDtypeStruct((8, width), f32),
        ],
        grid=(groups,),
        in_specs=[
            pl.BlockSpec(memory_space=pltpu.SMEM),
            full_spec(pairs),
            full_spec(scores),
            full_spec(mine),
            full_spec(theirs),
            row_spec((sentences, width)),
            row_spec((rows, 1, length)),
            row_spec((tile, width)),
            full_spec(gain_two),
        ],
        out_specs=[
            row_spec((tile, width)),
            column_spec((width, tile)),
            pl.BlockSpec((8, width), lambda step: (0, 0)),
        ],
        scratch_shapes=[
            pltpu.VMEM((groups, sentences, width), f32),
            pltpu.VMEM((groups, sentences, 128), f32),
        ],
        compiler_params=call_params(),
        cost_estimate=pl.CostEstimate(
            flops=100 * count * width, bytes_accessed=10 * count * width, transcendentals=count
        ),
    )(meta, pairs, scores, mine, theirs, pooled_low, seg_rows, second_sum, gain_two)


def backward_kernel(d_mid, slope, first_sum, gain_one, w_in, w_down, w_out):
    count, width = first_sum.shape
    ff_width = w_in.shape[1]
    tile = math.gcd(count, 256)
    chunk = 512

    def body(mid_ref, slope_ref, x_ref, g1_ref, win_ref, wdown_ref, wout_ref, *outs):
        up_ref, first_ref, low_ref, ctx_ref, wide_ref, grads_ref = outs

        @pl.when(pl.program_id(0) == 0)
        def _():
            grads_ref[...] = jnp.zeros_like(grads_ref)
            wide_ref[...] = jnp.zeros_like(wide_ref)

        d_hidden = mid_ref[...]
        mid_low = d_hidden.astype(bf16)
        for start in range(0, ff_width, chunk):
            part = slice(start, start + chunk)
            d_up = dot(mid_low, wdown_ref[part, :], 1, 1) * slope_ref[:, part].astype(f32)
            wide_ref[0:1, part] += jnp.sum(d_up, 0, keepdims=True)
            up_low = d_up.astype(bf16)
            up_ref[:, part] = up_low
            d_hidden = d_hidden + dot(up_low, win_ref[:, part], 1, 1)
        normed, inv_std = norm_parts(x_ref[...])
        d_first = norm_back(d_hidden, normed, inv_std, line(g1_ref))
        first_ref[...] = d_first
        first_low = d_first.astype(bf16)
        low_ref[...] = first_low
        ctx_ref[...] = dot(first_low, wout_ref[...], 1, 1).astype(bf16)
        grads_ref[0:1] += jnp.sum(d_first, 0, keepdims=True)
        grads_ref[1:2] += jnp.sum(d_hidden * normed, 0, keepdims=True)
        grads_ref[2:3] += jnp.sum(d_hidden, 0, keepdims=True)

    operands = [gain_one, w_in, w_down, w_out]
    return pl.pallas_call(
        body,
        out_shape=[
            jax.ShapeDtypeStruct((count, ff_width), bf16),
            jax.ShapeDtypeStruct((count, width), f32),
            jax.ShapeDtypeStruct((count, width), bf16),
            jax.ShapeDtypeStruct((count, width), bf16),
            jax.ShapeDtypeStruct((8, ff_width), f32),
            jax.ShapeDtypeStruct((8, width), f32),
        ],
        grid=(count // tile,),
        in_specs=[row_spec((tile, width)), row_spec((tile, ff_width)), row_spec((tile, width))]
        + [full_spec(entry) for entry in operands],
        out_specs=[
            row_spec((tile, ff_width)),
            row_spec((tile, width)),
            row_spec((tile, width)),
            row_spec((tile, width)),
            pl.BlockSpec((8, ff_width), lambda step: (0, 0)),
            pl.BlockSpec((8, width), lambda step: (0, 0)),
        ],
        compiler_params=call_params(),
        cost_estimate=pl.CostEstimate(
            flops=4 * count * width * ff_width + 2 * count * width * width,
            bytes_accessed=4 * count * ff_width + 16 * count * width + 4 * width * ff_width,
            transcendentals=0,
        ),
    )(d_mid, slope, first_sum, *operands)


def attention_back_kernel(qkv, d_context, seg_rows, part, parts, before=None):
    count, width = d_context.shape
    rows_all, length = seg_rows.shape[0], seg_rows.shape[2]
    rows = math.gcd(2, rows_all)
    tile = rows * length
    head_dim = width // HEADS
    scale = 1.0 / math.sqrt(head_dim)

    steps = rows_all // (rows * parts)
    base = part * steps

    def body(qkv_ref, dctx_ref, seg_ref, *rest):
        joint_ref, grads_ref = rest[-2:]

        @pl.when(pl.program_id(0) == 0)
        def _():
            grads_ref[...] = rest[1][...] if before else jnp.zeros_like(grads_ref)

        first = lax.broadcasted_iota(jnp.int32, (length, 2 * head_dim), 1) < head_dim
        zero = jnp.zeros((length, 2 * head_dim), bf16)

        def split(part):
            return jnp.concatenate([jnp.where(first, part, zero), jnp.where(first, zero, part)], 0)

        def beside(part):
            return jnp.concatenate([part[:length], part[length:]], 1)

        for row in range(rows):
            lines = slice(row * length, (row + 1) * length)
            mask = same_sentence(seg_ref[row])
            mask = jnp.concatenate([mask, mask], 0)
            for pair in range(HEADS // 2):
                at = pair * 2 * head_dim
                here = slice(at, at + 2 * head_dim)
                key_here = slice(width + at, width + at + 2 * head_dim)
                value_here = slice(2 * width + at, 2 * width + at + 2 * head_dim)
                query = split(qkv_ref[lines, here])
                key = qkv_ref[lines, key_here]
                grad = split(dctx_ref[lines, here])
                score = jnp.where(mask, dot(query, key, 1, 1) * scale, -1e30)
                expo = jnp.exp(score - jnp.max(score, -1, keepdims=True))
                attn = expo * (1.0 / jnp.sum(expo, -1, keepdims=True))
                d_attn = dot(grad, qkv_ref[lines, value_here], 1, 1)
                weighted = attn * d_attn
                d_score = weighted - attn * jnp.sum(weighted, -1, keepdims=True)
                d_score = d_score.astype(bf16)
                d_value = dot(attn.astype(bf16), grad, 0, 0)
                d_key = dot(d_score, query, 0, 0) * scale
                d_query = dot(beside(d_score), split(key)) * scale
                joint_ref[lines, here] = d_query.astype(bf16)
                joint_ref[lines, key_here] = d_key.astype(bf16)
                joint_ref[lines, value_here] = d_value.astype(bf16)
                grads_ref[0:1, here] += jnp.sum(d_query, 0, keepdims=True)
                grads_ref[1:2, here] += jnp.sum(d_value, 0, keepdims=True)

    return pl.pallas_call(
        body,
        out_shape=[
            jax.ShapeDtypeStruct((count, 3 * width), bf16),
            jax.ShapeDtypeStruct((8, width), f32),
        ],
        grid=(steps,),
        in_specs=[
            pl.BlockSpec((tile, 3 * width), lambda step: (base + step, 0)),
            pl.BlockSpec((tile, width), lambda step: (base + step, 0)),
            pl.BlockSpec((rows, 1, length), lambda step: (base + step, 0, 0)),
        ]
        + ([pl.BlockSpec(memory_space=pl.ANY), full_spec(before[1])] if before else []),
        out_specs=[
            pl.BlockSpec((tile, 3 * width), lambda step: (base + step, 0)),
            pl.BlockSpec((8, width), lambda step: (0, 0)),
        ],
        input_output_aliases={3: 0} if before else {},
        compiler_params=call_params(),
        cost_estimate=pl.CostEstimate(
            flops=14 * count * width * length // parts,
            bytes_accessed=14 * count * width // parts,
            transcendentals=count * HEADS * length // parts,
        ),
    )(qkv, d_context, seg_rows, *(before or ()))


def on_device(
    tokens,
    segments,
    pairs,
    scores,
    w_qkv,
    b_query,
    b_value,
    w_out,
    b_out,
    gain_one,
    shift_one,
    w_in,
    b_in,
    w_down,
    b_down,
    gain_two,
    shift_two,
):
    dp_size = lax.axis_size("dp")
    core, table = place_tables(dp_size)
    place = jnp.stack([lax.axis_index("tower"), lax.axis_index("dp")]).astype(jnp.int32)
    flat_rows = tokens[0]
    seg_rows = segments[0][:, None, :]
    width = flat_rows.shape[1]
    ff_width = w_in.shape[1]
    qkv, context_turned, tokens_turned, first_sum = attention_kernel(
        flat_rows, seg_rows, w_qkv, b_query, b_value, w_out, b_out
    )
    hidden_turned, act, slope, second_sum, output_rows, pooled_low = forward_kernel(
        first_sum, seg_rows, gain_one, shift_one, w_in, b_in, w_down, b_down, gain_two, shift_two
    )
    mine, theirs, spans = gather_pooled(pooled_low, dp_size)
    d_mid, d_mid_turned, grads_two = loss_kernel(
        place,
        pairs.reshape(-1, 128),
        scores.reshape(-1, 128),
        mine,
        theirs,
        pooled_low,
        seg_rows,
        second_sum,
        gain_two,
        spans,
    )

    def own_half(rhs, turned, *more):
        return grad_half(turned, rhs, core, table[0], f32, *more)

    def other_half(rhs, turned, *more):
        return grad_half(turned, rhs, 1 - core, table[1], bf16, *more)

    down = Sum(other_half(act, d_mid_turned), dp_size)
    beside(lambda entry: own_half(act, entry), d_mid_turned, down, keeps=down)
    d_up_low, d_first, d_first_low, d_context, grads_wide, grads_one = beside(
        lambda entry: backward_kernel(entry, slope, first_sum, gain_one, w_in, w_down, w_out),
        d_mid,
        down,
    )
    out_pair = (context_turned, d_first_low)
    sent = beside(lambda entry: other_half(entry, hidden_turned, out_pair), d_up_low, down)
    feed = Sum(sent, dp_size)
    beside(
        lambda entry: own_half(entry, hidden_turned, out_pair), d_up_low, down, feed, keeps=feed
    )
    half_joint = beside(
        lambda entry: attention_back_kernel(qkv, entry, seg_rows, 0, 2), d_context, down, feed
    )
    d_joint, grads_attn = beside(
        lambda entry: attention_back_kernel(qkv, d_context, seg_rows, 1, 2, entry),
        half_joint,
        down,
        feed,
    )
    smalls = [
        (grads_attn, 0),
        (grads_attn, 1),
        (grads_one, 0),
        (grads_one, 1),
        (grads_one, 2),
        (grads_wide, 0),
        (grads_two, 2),
        (grads_two, 0),
        (grads_two, 1),
    ]
    sent = beside(
        lambda entry: other_half(entry, tokens_turned, None, smalls), d_joint, down, feed
    )
    joint = Sum(sent, dp_size)
    beside(
        lambda entry: own_half(entry, tokens_turned, None, smalls),
        d_joint,
        down,
        feed,
        joint,
        keeps=joint,
    )
    grad_tokens = beside(
        lambda entry: d_first
        + jnp.einsum("ne,de->nd", entry, w_qkv, preferred_element_type=f32),
        d_joint,
        down,
        feed,
        joint,
    )
    grad_w_down = finish_turned(*down.run(), core, table)
    grad_w_in, grad_w_out = finish(*feed.run(), core, table, [ff_width // 2, width // 2])
    small_widths = [width] * 5 + [ff_width] + [width] * 3
    grad_w_qkv, *smalls = finish(*joint.run(), core, table, [3 * width // 2], small_widths)
    return (
        output_rows[None],
        grad_tokens[None],
        grad_w_qkv,
        smalls[0],
        smalls[1],
        grad_w_out,
        smalls[2],
        smalls[3],
        smalls[4],
        grad_w_in,
        smalls[5],
        grad_w_down,
        smalls[6],
        smalls[7],
        smalls[8],
    )


def solution(mesh):
    return jax.shard_map(
        on_device,
        mesh=mesh,
        in_specs=(
            P("tower", "dp", None),
            P("tower", "dp", None),
            P(),
            P(),
            P(),
            P(),
            P(),
            P(),
            P(),
            P(),
            P(),
            P(),
            P(),
            P(),
            P(),
            P(),
            P(),
        ),
        out_specs=(
            P("tower", "dp", None),
            P("tower", "dp", None),
            P(),
            P(),
            P(),
            P(),
            P(),
            P(),
            P(),
            P(),
            P(),
            P(),
            P(),
            P(),
            P(),
        ),
        check_vma=False,
    )
```
